512 devices in a mesh: dp: 16 (over x, y_hi), expert: 32 (over z, y_lo, core).
Axes of the slice: x: 4, y: 8 (y_hi: 4, y_lo: 2; y = y_hi * 2 + y_lo), z: 8, core: 2. Of those that a mesh axis runs over, the one named last changes fastest.
Arguments:
- patches: bfloat16 [65536, 1024], P(('dp', 'expert')), may hold values from -6 to 6
- expert_ids: int32 [65536, 2], P(('dp', 'expert')), may hold values from 0 to 31, all different within a row; in each aligned block of 128 rows (0 to 127, 128 to 255, ...) at most 16 rows name the same one
- gate_weights: float32 [65536, 2], P(('dp', 'expert')), may hold values from 0.2 to 1
- conv_weight: float32 [49, 1024], replicated, may hold values from -2 to 2
- conv_bias: float32 [1024], replicated, may hold values from -6 to 6
- ln_gain: float32 [1024], replicated, may hold values from 0.1 to 1.9
- ln_shift: float32 [1024], replicated, may hold values from -6 to 6
- w_in: bfloat16 [32, 1024, 1024], P('expert', 'dp'), may hold values from -0.1875 to 0.1875
- w_out: bfloat16 [32, 1024, 1024], P('expert', 'dp'), may hold values from -0.1875 to 0.1875
- grad_mixed: bfloat16 [65536, 1024], P(('dp', 'expert')), may hold values from -6 to 6
Outputs:
- mixed: bfloat16 [65536, 1024], P(('dp', 'expert'))
- grad_input: float32 [65536, 1024], P(('dp', 'expert'))
- grad_w_in: float32 [32, 1024, 1024], P('expert', 'dp')
- grad_w_out: float32 [32, 1024, 1024], P('expert', 'dp')
The draws below stay inside these ranges and needn't reach their ends.
Inputs may be any that keep to these rules, and one draw needn't show every extreme that they name: `expert_ids`: the two ids of a row differ. Within the 128 rows of one device no expert is named more than 16 times, a bound that some block reaches in every draw.
All inputs are finite; a program needn't handle non-finite values.
Results may differ from the reference program's by a relative error of at most 0.013.
Values may be sent and summed in bfloat16 or wider, within the bound.
No kernel may reach another device: no remote copies, remote signals or barrier semaphores. Data moves between devices by JAX's collectives and lax.ppermute only.
A program may use at most 64 MiB of HBM per device.

```python
import math
from functools import partial
import jax
import jax.numpy as jnp
import numpy as np
from jax import lax

D = 1024
EXP_HID = 1024
KSIZE = 7
TOP = 2
IMG_W = 16
IMG_H = 8
TOK_DEV = 128
EXPERTS = 32
CAP = 16
TOKENS = 65536
N_DP = 16
N_EXPERT = 32


def steps_of(stream_key, extent, shards, least, high):
    def one(axis_at, parts):
        heights = jax.random.uniform(jax.random.fold_in(jax.random.fold_in(stream_key, 6), axis_at), (parts,), jnp.float32, least / len(shards), high / len(shards))
        return jnp.repeat(jnp.exp(heights), extent[axis_at] // parts).reshape((-1,) + (1,) * (len(extent) - axis_at - 1))

    gain = one(*shards[0])
    for cut in shards[1:]:
        gain = gain * one(*cut)
    return gain


def deal_out(own_key, own, number, rows, number_of, top, reach, skew):
    order = jax.random.permutation(own_key, number_of)
    heavy_load, usual = portions_of(number_of, rows * top, reach, skew, True), portions_of(number_of, rows * top, reach, skew, False)
    places = jnp.arange(number_of)

    def named(sizes, turn):
        used = int((sizes > 0).sum())
        fixed = max(1, used // 4)
        moved = fixed + (places - fixed + turn * (used - fixed)) % max(1, number_of - fixed)
        return jnp.zeros((number_of,), jnp.int32).at[order[jnp.where(places < fixed, places, moved)]].set(jnp.asarray(sizes, jnp.int32))

    sizes = jnp.where(number % 4 == 0, named(heavy_load, number // 4), named(usual, number - number // 4 - 1))
    mixed = jax.random.permutation(jax.random.fold_in(own, 3), number_of)
    giver, receiver = mixed[0:number_of // 2 * 2:2], mixed[1:number_of // 2 * 2:2]
    slack = jnp.minimum(sizes[giver] - 1, reach - sizes[receiver]) // 2
    slack = jnp.where((giver == order[0]) | (receiver == order[0]) | (sizes[receiver] == 0), 0, jnp.maximum(slack, 0))
    moved = jax.random.randint(jax.random.fold_in(own, 4), (number_of // 2,), 0, 1 << 20) % (slack + 1)
    sizes = sizes.at[giver].add(-moved).at[receiver].add(moved)
    labels = jnp.searchsorted(jnp.cumsum(sizes), jnp.arange(rows * top), side="right").astype(jnp.int32)
    listing = labels.reshape(top, rows).T
    listing = listing[jax.random.permutation(jax.random.fold_in(own, 1), rows)]
    turn = jax.random.randint(jax.random.fold_in(own, 2), (rows, 1), 0, top)
    return jnp.take_along_axis(listing, (jnp.arange(top)[None, :] + turn) % top, axis=1)


def portions_of(count, total, bound, lean, full):
    portions = [(1 << 20) // math.isqrt(standing ** lean) + 1 for standing in range(1, count + 1)]
    largest = bound if full else min(bound, max(-(-total // count), total * portions[0] // sum(portions)))
    least = 1 if total - largest >= count - 1 else 0
    holding, surplus = [largest] + [least] * (count - 1), total - largest - least * (count - 1)
    while surplus > 0:
        movable = [i for i in range(1, count) if holding[i] < largest] or [i for i in range(1, count) if holding[i] < bound]
        pool, left = sum([portions[i] for i in movable]), surplus
        for i in movable:
            extra = min(bound - holding[i], max(1, left * portions[i] // pool), surplus)
            holding[i] = holding[i] + extra
            surplus = surplus - extra
    return np.array(holding)


def bell_draw(own_key, shape, deviation, most, shards=(), kind=jnp.bfloat16):
    drawn = deviation * jax.random.normal(own_key, shape, jnp.float32)
    if shards:
        drawn = drawn * steps_of(own_key, shape, shards, -0.22, 0.18)
    return jnp.clip(drawn, -most, most).astype(kind)


def setup_inputs(seed: int = 0) -> dict:
    keys = jax.random.split(jax.random.key(seed), 11)
    patches = bell_draw(keys[0], (TOKENS, D), 1.0, 6.0, ((0, 512),))
    expert_ids_keys = jax.random.split(jax.random.fold_in(keys[1], 1), TOKENS // TOK_DEV)
    expert_ids_turns = jax.random.permutation(jax.random.fold_in(keys[1], 3), TOKENS // TOK_DEV)
    expert_ids = jax.vmap(lambda own, number: deal_out(jax.random.fold_in(keys[1], 2), own, number, TOK_DEV, EXPERTS, TOP, CAP, 2))(expert_ids_keys, expert_ids_turns).reshape((TOKENS, TOP))
    gate_weights = jnp.clip(0.2 + 0.8 * jax.random.uniform(keys[2], (TOKENS, TOP), jnp.float32) ** steps_of(keys[2], (TOKENS, TOP), ((0, 512),), -0.2, 0.2), 0.2, 1.0)
    conv_weight = bell_draw(keys[3], (KSIZE * KSIZE, D), 0.15, 2.0, (), jnp.float32)
    conv_bias = bell_draw(keys[4], (D,), 0.5, 6.0, (), jnp.float32)
    ln_gain = jnp.clip(1.0 + 0.18 * jax.random.normal(keys[5], (D,), jnp.float32), 0.1, 1.9)
    ln_shift = bell_draw(keys[6], (D,), 0.5, 6.0, (), jnp.float32)
    w_in = bell_draw(keys[7], (EXPERTS, D, EXP_HID), D ** -0.5, 0.1875, ((0, 32), (1, 16)))
    w_out = bell_draw(keys[8], (EXPERTS, D, EXP_HID), EXP_HID ** -0.5, 0.1875, ((0, 32), (1, 16)))
    grad_mixed = bell_draw(keys[9], (TOKENS, D), 1.0, 6.0, ((0, 512),))
    return dict(patches=patches, expert_ids=expert_ids, gate_weights=gate_weights, conv_weight=conv_weight, conv_bias=conv_bias, ln_gain=ln_gain, ln_shift=ln_shift, w_in=w_in, w_out=w_out, grad_mixed=grad_mixed)


EPS = 1e-06

def front(images, conv_weight, conv_bias, ln_gain, ln_shift):
    half = KSIZE // 2
    padded = jnp.pad(images, ((0, 0), (half, half), (half, half), (0, 0)))
    total = jnp.zeros_like(images) + conv_bias
    for row in range(KSIZE):
        for col in range(KSIZE):
            total = total + padded[:, row:row + IMG_H, col:col + IMG_W, :] * conv_weight[row * KSIZE + col]
    mean = lax.optimization_barrier(jnp.mean(total, axis=-1, keepdims=True))
    centred = total - mean
    spread = lax.optimization_barrier(jnp.mean(centred * centred, axis=-1, keepdims=True))
    return centred * lax.rsqrt(spread + EPS) * ln_gain + ln_shift

def slot_positions(ids, capacity, count):
    flat = ids.reshape(-1)
    table = (flat[:, None] == jnp.arange(count, dtype=jnp.int32)[None, :]).astype(jnp.int32)
    earlier = (jnp.cumsum(table, axis=0) - table).astype(jnp.int32)
    slots = lax.optimization_barrier(jnp.sum(earlier * table, axis=1)).astype(jnp.int32)
    return (flat * capacity + slots).astype(jnp.int32).reshape(ids.shape)

def to_experts(sent):
    members = sent.shape[0]
    return sent.reshape(members, EXPERTS, CAP, D).transpose(1, 0, 2, 3).reshape(EXPERTS, members * CAP, D)

def to_sources(rows):
    members = rows.shape[1] // CAP
    return rows.reshape(EXPERTS, members, CAP, D).transpose(1, 0, 2, 3).reshape(members, EXPERTS * CAP, D)

def one_expert(inputs):
    rows, grads, weight_in, weight_out = inputs
    hidden_pre = jnp.dot(rows, weight_in, preferred_element_type=jnp.float32)
    hidden = jax.nn.gelu(hidden_pre).astype(jnp.bfloat16)
    result = jnp.dot(hidden, weight_out.T, preferred_element_type=jnp.float32).astype(jnp.bfloat16)
    raw = jnp.dot(grads, weight_out, preferred_element_type=jnp.float32)
    grad_hidden = jax.vjp(jax.nn.gelu, hidden_pre)[1](raw)[0].astype(jnp.bfloat16)
    grad_back = jnp.dot(grad_hidden, weight_in.T, preferred_element_type=jnp.float32).astype(jnp.bfloat16)
    part_in = jnp.dot(rows.T, grad_hidden, preferred_element_type=jnp.float32).astype(jnp.bfloat16)
    part_out = jnp.dot(grads.T, hidden, preferred_element_type=jnp.float32).astype(jnp.bfloat16)
    return (result, grad_back, part_in.astype(jnp.float32), part_out.astype(jnp.float32))

def reference(patches, expert_ids, gate_weights, conv_weight, conv_bias, ln_gain, ln_shift, w_in, w_out, grad_mixed):
    members = N_EXPERT
    shaped = partial(front, conv_weight=conv_weight, conv_bias=conv_bias, ln_gain=ln_gain, ln_shift=ln_shift)
    all_slots = jnp.arange(EXPERTS * CAP, dtype=jnp.int32)

    def one_group(carry, inputs):
        patch_g, ids_g, gate_g, cot_g = inputs
        images = patch_g.astype(jnp.float32).reshape(members, IMG_H, IMG_W, D)
        pre, back_front = jax.vjp(shaped, images)
        normed = pre.reshape(members, TOK_DEV, D).astype(jnp.bfloat16)
        ids = ids_g.reshape(members, TOK_DEV, TOP)
        positions = jax.vmap(lambda block: slot_positions(block, CAP, EXPERTS))(ids)
        gates = gate_g.reshape(members, TOK_DEV, TOP)
        hits = (positions[:, None, :, :] == all_slots[None, :, None, None]).astype(jnp.float32)
        select = lax.optimization_barrier(jnp.sum(hits, axis=-1))
        sent = jnp.einsum('mst,mtd->msd', select, normed.astype(jnp.float32)).astype(jnp.bfloat16)
        gate_select = lax.optimization_barrier(jnp.sum(hits * gates[:, None, :, :], axis=-1))
        cot = cot_g.reshape(members, TOK_DEV, D).astype(jnp.float32)
        grad_sent = jnp.einsum('mst,mtd->msd', gate_select, cot, precision=lax.Precision.HIGHEST).astype(jnp.bfloat16)
        outs, grad_back, part_in, part_out = lax.map(one_expert, (to_experts(sent), to_experts(grad_sent), w_in, w_out))
        back = to_sources(outs)
        grad_ret = to_sources(grad_back)
        picked = jax.vmap(lambda table, pos: jnp.take(table, pos.reshape(-1), axis=0))(back, positions)
        picked = picked.reshape(members, TOK_DEV, TOP, D).astype(jnp.float32)
        combined = lax.optimization_barrier(jnp.sum(picked * gates[..., None], axis=2))
        mixed = (patch_g.astype(jnp.float32).reshape(members, TOK_DEV, D) + combined).astype(jnp.bfloat16)
        picked_grad = jax.vmap(lambda table, pos: jnp.take(table, pos.reshape(-1), axis=0))(grad_ret, positions)
        grad_normed = lax.optimization_barrier(jnp.sum(picked_grad.reshape(members, TOK_DEV, TOP, D).astype(jnp.float32), axis=2))
        grad_front = back_front(grad_normed.reshape(members, IMG_H, IMG_W, D))[0]
        grad_input = cot + grad_front.reshape(members, TOK_DEV, D)
        total_in, total_out = carry
        return ((total_in + part_in, total_out + part_out), (mixed.reshape(members * TOK_DEV, D), grad_input.reshape(members * TOK_DEV, D)))
    start = (jnp.zeros((EXPERTS, D, EXP_HID), jnp.float32), jnp.zeros((EXPERTS, D, EXP_HID), jnp.float32))
    inputs = (patches.reshape(N_DP, members * TOK_DEV, D), expert_ids.reshape(N_DP, members * TOK_DEV, TOP), gate_weights.reshape(N_DP, members * TOK_DEV, TOP), grad_mixed.reshape(N_DP, members * TOK_DEV, D))
    (grad_w_in, grad_w_out), (mixed, grad_input) = lax.scan(one_group, start, inputs)
    return (mixed.reshape(TOKENS, D), grad_input.reshape(TOKENS, D), grad_w_in, grad_w_out)
```

```python
import jax
import jax.numpy as jnp
from jax import lax
from jax.experimental import pallas as pl
from jax.experimental.pallas import tpu as pltpu
from jax.sharding import Mesh, PartitionSpec as P


KSIZE = 7
TOP = 2
IMG_W = 16
IMG_H = 8
EPS = 1e-06
EXPERTS = 32
CAP = 16
TOK = 128
SLOTS = EXPERTS * CAP
LANES = 128
F32 = jnp.float32
BF16 = jnp.bfloat16
MIB = 1 << 20

VMEM = pl.BlockSpec(memory_space=pltpu.VMEM)


def dot(a, b):
    return jnp.dot(a, b, preferred_element_type=F32)


def iota(shape, dim):
    return lax.broadcasted_iota(jnp.int32, shape, dim)


def slot_selects(ids_ref):
    turned = [
        jnp.broadcast_to(ids_ref[:, k : k + 1].astype(F32), (TOK, TOK)).T.astype(jnp.int32)
        for k in range(TOP)
    ]
    hot = [row[:EXPERTS] == iota((EXPERTS, TOK), 0) for row in turned]
    table = (hot[0] | hot[1]).astype(F32).astype(BF16)
    before = (iota((TOK, TOK), 0) < iota((TOK, TOK), 1)).astype(F32).astype(BF16)
    earlier = dot(table, before)
    out = []
    for k in range(TOP):
        slot = jnp.sum(jnp.where(hot[k], earlier, 0.0), axis=0, keepdims=True)
        position = turned[k][:1] * CAP + slot.astype(jnp.int32)
        out.append(iota((SLOTS, TOK), 0) == position)
    return out


def patch_selects(ids_ref):
    hot = [ids_ref[:, k : k + 1] == iota((TOK, EXPERTS), 1) for k in range(TOP)]
    table = (hot[0] | hot[1]).astype(F32).astype(BF16)
    before = (iota((TOK, TOK), 1) < iota((TOK, TOK), 0)).astype(F32).astype(BF16)
    earlier = dot(before, table)
    out = []
    for k in range(TOP):
        slot = jnp.sum(jnp.where(hot[k], earlier, 0.0), axis=1, keepdims=True)
        position = ids_ref[:, k : k + 1] * CAP + slot.astype(jnp.int32)
        out.append(iota((TOK, SLOTS), 1) == position)
    return out


def as_bf16(mask):
    return mask.astype(F32).astype(BF16)


def send_grads_kernel(ids_ref, gates_ref, cot_ref, out_ref):
    select = slot_selects(ids_ref)
    cot = cot_ref[...].astype(F32)
    first = (gates_ref[:, 0:1] * cot).astype(BF16)
    second = (gates_ref[:, 1:2] * cot).astype(BF16)
    out_ref[...] = (dot(as_bf16(select[0]), first) + dot(as_bf16(select[1]), second)).astype(BF16)


def depthwise(padded, taps_ref, flip, start, put):
    half = KSIZE // 2

    def chunk(c, _):
        lanes = pl.ds(pl.multiple_of(c * LANES, LANES), LANES)
        total = start(lanes)
        for col in range(KSIZE):
            begin = 8 + col - half
            shifted = padded[:, begin : begin + IMG_W, lanes]
            for row in range(KSIZE):
                tap = (KSIZE - 1 - row) * KSIZE + KSIZE - 1 - col if flip else row * KSIZE + col
                weight = taps_ref[tap : tap + 1, lanes]
                total = total + shifted[row : row + IMG_H] * weight[None]
        put(lanes, total)
        return 0

    lax.fori_loop(0, padded.shape[2] // LANES, chunk, 0)


def front_kernel(
    ids_ref, x_ref, taps_ref, bias_ref, gain_ref, shift_ref, sent_ref, xhat_ref, rstd_ref, padded, total
):
    width = x_ref.shape[1]
    half = KSIZE // 2
    padded[...] = jnp.zeros_like(padded)
    padded[half : half + IMG_H, 8 : 8 + IMG_W, :] = (
        x_ref[...].astype(F32).reshape(IMG_H, IMG_W, width)
    )

    def start(lanes):
        return jnp.broadcast_to(bias_ref[:, lanes][None], (IMG_H, IMG_W, LANES))

    def put(lanes, value):
        total[:, lanes] = value.reshape(TOK, LANES)

    depthwise(padded, taps_ref, False, start, put)
    conv = total[...]
    mean = jnp.sum(conv, axis=1, keepdims=True) * (1.0 / width)
    centred = conv - mean
    spread = jnp.sum(centred * centred, axis=1, keepdims=True) * (1.0 / width)
    rstd = lax.rsqrt(spread + EPS)
    xhat = centred * rstd
    xhat_ref[...] = xhat
    rstd_ref[...] = jnp.broadcast_to(rstd, (TOK, LANES))
    normed = (xhat * gain_ref[...] + shift_ref[...]).astype(BF16)
    select = slot_selects(ids_ref)
    sent_ref[...] = dot(as_bf16(select[0] | select[1]), normed).astype(BF16)


def back_kernel(
    ids_ref, back_ref, xhat_ref, rstd_ref, gain_ref, taps_ref, cot_ref, out_ref, padded
):
    width = xhat_ref.shape[1]
    half = KSIZE // 2
    select = patch_selects(ids_ref)
    grad = dot(as_bf16(select[0] | select[1]), back_ref[...])
    grad = grad * gain_ref[...]
    xhat = xhat_ref[...]
    mean = jnp.sum(grad, axis=1, keepdims=True) * (1.0 / width)
    along = jnp.sum(grad * xhat, axis=1, keepdims=True) * (1.0 / width)
    grad = rstd_ref[:, 0:1] * (grad - mean - xhat * along)
    padded[...] = jnp.zeros_like(padded)
    padded[half : half + IMG_H, 8 : 8 + IMG_W, :] = grad.reshape(IMG_H, IMG_W, width)

    def start(lanes):
        return jnp.zeros((IMG_H, IMG_W, LANES), F32)

    def put(lanes, value):
        out_ref[:, lanes] = cot_ref[:, lanes].astype(F32) + value.reshape(TOK, LANES)

    depthwise(padded, taps_ref, True, start, put)


def mix_kernel(ids_ref, gates_ref, back_ref, x_ref, out_ref):
    select = patch_selects(ids_ref)
    rows = back_ref[...]
    combined = gates_ref[:, 0:1] * dot(as_bf16(select[0]), rows)
    combined = combined + gates_ref[:, 1:2] * dot(as_bf16(select[1]), rows)
    out_ref[...] = (x_ref[...].astype(F32) + combined).astype(BF16)


def contract_last(left, right):
    return lax.dot_general(left, right, (((1,), (1,)), ((), ())), preferred_element_type=F32)


def contract_first(left, right):
    return lax.dot_general(left, right, (((0,), (0,)), ((), ())), preferred_element_type=F32)


SQRT_2_OVER_PI = 0.7978845608028654


def expert_kernel(rows_ref, grads_ref, w_in_ref, w_out_ref, back_ref, hidden_ref, gh_ref, total):
    step = pl.program_id(0)
    pre = dot(rows_ref[...], w_in_ref[...])
    raw = dot(grads_ref[...], w_out_ref[...])
    square = pre * pre
    t = jnp.tanh(SQRT_2_OVER_PI * (pre + 0.044715 * (pre * square)))
    cdf = 0.5 * (1.0 + t)
    hidden_ref[...] = (pre * cdf).astype(BF16)
    slope = cdf + pre * (0.5 * (1.0 - t * t)) * (
        SQRT_2_OVER_PI * (1.0 + (3 * 0.044715) * square)
    )
    gh = (raw * slope).astype(BF16)
    gh_ref[...] = gh
    part = contract_last(gh, w_in_ref[...])

    @pl.when(step == 0)
    def _():
        total[...] = part

    @pl.when(step > 0)
    def _():
        total[...] += part

    @pl.when(step == pl.num_programs(0) - 1)
    def _():
        back_ref[...] = total[...].astype(BF16)


def terms_kernel(rows_ref, grads_ref, hidden_ref, gh_ref, out_ref):
    hid = hidden_ref.shape[1]
    out_ref[:, :hid] = contract_first(rows_ref[...], gh_ref[...]).astype(BF16)
    out_ref[:, hid:] = contract_first(grads_ref[...], hidden_ref[...]).astype(BF16)


def result_kernel(hidden_ref, w_out_ref, out_ref):
    out_ref[...] = contract_last(hidden_ref[...], w_out_ref[...]).astype(BF16)


def params(mib=16):
    return pltpu.CompilerParams(vmem_limit_bytes=mib * MIB)


def cost(flops, nbytes):
    return pl.CostEstimate(flops=int(flops), bytes_accessed=int(nbytes), transcendentals=0)


def shape(dims, dtype):
    return jax.ShapeDtypeStruct(dims, dtype)


def send_grads(ids, gates, cot):
    width = cot.shape[1]
    return pl.pallas_call(
        send_grads_kernel,
        out_shape=shape((SLOTS, width), BF16),
        in_specs=[VMEM] * 3,
        out_specs=VMEM,
        compiler_params=params(),
        cost_estimate=cost(4 * SLOTS * TOK * width, 2 * SLOTS * width),
        name="send_grads",
    )(ids, gates, cot)


def front(ids, x, taps, bias, gain, shift):
    width = x.shape[1]
    return pl.pallas_call(
        front_kernel,
        out_shape=(
            shape((SLOTS, width), BF16),
            shape((TOK, width), F32),
            shape((TOK, LANES), F32),
        ),
        in_specs=[VMEM] * 6,
        out_specs=[VMEM] * 3,
        scratch_shapes=[
            pltpu.VMEM((IMG_H + KSIZE - 1, IMG_W + 16, width), F32),
            pltpu.VMEM((TOK, width), F32),
        ],
        compiler_params=params(),
        cost_estimate=cost(100 * TOK * width * 20, 4 * SLOTS * width),
        name="front",
    )(ids, x, taps, bias.reshape(1, width), gain.reshape(1, width), shift.reshape(1, width))


def back(ids, grad_rows, xhat, rstd, gain, taps, cot):
    width = cot.shape[1]
    return pl.pallas_call(
        back_kernel,
        out_shape=shape((TOK, width), F32),
        in_specs=[VMEM] * 7,
        out_specs=VMEM,
        scratch_shapes=[pltpu.VMEM((IMG_H + KSIZE - 1, IMG_W + 16, width), F32)],
        compiler_params=params(),
        cost_estimate=cost(100 * TOK * width * 20, 4 * SLOTS * width),
        name="back",
    )(ids, grad_rows, xhat, rstd, gain.reshape(1, width), taps, cot)


def mix(ids, gates, rows, x):
    width = x.shape[1]
    return pl.pallas_call(
        mix_kernel,
        out_shape=shape((TOK, width), BF16),
        in_specs=[VMEM] * 4,
        out_specs=VMEM,
        compiler_params=params(),
        cost_estimate=cost(4 * SLOTS * TOK * width, 2 * SLOTS * width),
        name="mix",
    )(ids, gates, rows, x)


def expert(rows, grads, weights):
    count, width = rows.shape
    hid = weights.shape[1] // 2
    block = 256
    steps = hid // block
    whole = pl.BlockSpec((count, width), lambda j: (0, 0))
    return pl.pallas_call(
        expert_kernel,
        grid=(steps,),
        out_shape=(
            shape((count, width), BF16),
            shape((count, hid), BF16),
            shape((count, hid), BF16),
        ),
        in_specs=[
            whole,
            whole,
            pl.BlockSpec((width, block), lambda j: (0, j)),
            pl.BlockSpec((width, block), lambda j: (0, j + steps)),
        ],
        out_specs=[
            whole,
            pl.BlockSpec((count, block), lambda j: (0, j)),
            pl.BlockSpec((count, block), lambda j: (0, j)),
        ],
        scratch_shapes=[pltpu.VMEM((count, width), F32)],
        compiler_params=params(32),
        cost_estimate=cost(6 * count * width * hid, 4 * MIB),
        name="expert",
    )(rows, grads, weights, weights)


def terms(rows, grads, hidden, gh):
    count, width = rows.shape
    hid = hidden.shape[1]
    block = 256
    part = pl.BlockSpec((count, block), lambda i: (0, i))
    whole = pl.BlockSpec((count, hid), lambda i: (0, 0))
    return pl.pallas_call(
        terms_kernel,
        grid=(width // block,),
        out_shape=shape((width, 2 * hid), BF16),
        in_specs=[part, part, whole, whole],
        out_specs=pl.BlockSpec((block, 2 * hid), lambda i: (i, 0)),
        compiler_params=params(32),
        cost_estimate=cost(4 * count * width * hid, 4 * MIB),
        name="terms",
    )(rows, grads, hidden, gh)


def result_rows(hidden, weights):
    count, hid = hidden.shape
    width = weights.shape[0]
    block = 256
    return pl.pallas_call(
        result_kernel,
        grid=(width // block,),
        out_shape=shape((count, width), BF16),
        in_specs=[
            pl.BlockSpec((count, hid), lambda i: (0, 0)),
            pl.BlockSpec((block, hid), lambda i: (i, 1)),
        ],
        out_specs=pl.BlockSpec((count, block), lambda i: (0, i)),
        compiler_params=params(),
        cost_estimate=cost(2 * count * width * hid, 4 * MIB),
        name="result",
    )(hidden, weights)


def exchange(rows, axes):
    count, width = rows.shape
    out = lax.all_to_all(
        rows.reshape(EXPERTS, CAP, width), axes, split_axis=0, concat_axis=0, tiled=True
    )
    return out.reshape(count, width)


def scatter_sum(partial):
    over_x = lax.psum_scatter(partial, "x", scatter_dimension=0, tiled=True)
    parts = lax.axis_size("yh")
    own = lax.axis_index("yh")
    height = over_x.shape[0] // parts

    def piece(which):
        return lax.dynamic_slice_in_dim(over_x, lax.rem(which, parts) * height, height, axis=0)

    total = piece(own).astype(F32)
    for k in (2, 1, 3):
        got = lax.ppermute(piece(own + k), "yh", [(i, (i + k) % parts) for i in range(parts)])
        total = total + got.astype(F32)
    return total


def local(
    patches,
    expert_ids,
    gate_weights,
    conv_weight,
    conv_bias,
    ln_gain,
    ln_shift,
    w_in,
    w_out,
    grad_mixed,
):
    hid = w_in.shape[2]
    dp = ("x", "yh")
    ep = ("z", "yl", "core")
    weights = lax.all_gather(jnp.concatenate([w_in, w_out], axis=2), dp, axis=1, tiled=True)[0]

    gated = send_grads(expert_ids, gate_weights, grad_mixed)
    grads = exchange(gated, ep)
    sent, xhat, rstd = front(
        expert_ids, patches, conv_weight, conv_bias, ln_gain, ln_shift
    )
    rows = exchange(sent, ep)

    grad_back, hidden, gh = expert(rows, grads, weights)
    grad_rows = exchange(grad_back, ep)
    partial = terms(rows, grads, hidden, gh)
    total = scatter_sum(partial)
    result = result_rows(hidden, weights)
    returned = exchange(result, ep)
    grad_input = back(
        expert_ids, grad_rows, xhat, rstd, ln_gain, conv_weight, grad_mixed
    )
    mixed = mix(expert_ids, gate_weights, returned, patches)
    return (mixed, grad_input, total[:, :hid][None], total[:, hid:][None])


def solution(mesh):
    fine = Mesh(mesh.devices.reshape(4, 4, 8, 2, 2), ("x", "yh", "z", "yl", "core"))
    dp = ("x", "yh")
    ep = ("z", "yl", "core")
    rows = P(dp + ep, None)
    weight = P(ep, dp, None)
    return jax.shard_map(
        local,
        mesh=fine,
        in_specs=(rows, rows, rows, P(), P(), P(), P(), weight, weight, rows),
        out_specs=(rows, rows, weight, weight),
        check_vma=False,
    )
```

```python
import jax
import jax.numpy as jnp
from jax import lax
from jax.experimental import pallas as pl
from jax.experimental.pallas import tpu as pltpu
from jax.sharding import Mesh, PartitionSpec as P


KSIZE = 7
TOP = 2
IMG_W = 16
IMG_H = 8
EPS = 1e-06
EXPERTS = 32
CAP = 16
TOK = 128
SLOTS = EXPERTS * CAP
LANES = 128
F32 = jnp.float32
BF16 = jnp.bfloat16
MIB = 1 << 20

VMEM = pl.BlockSpec(memory_space=pltpu.VMEM)


def dot(a, b):
    return jnp.dot(a, b, preferred_element_type=F32)


def iota(shape, dim):
    return lax.broadcasted_iota(jnp.int32, shape, dim)


def slot_selects(ids_ref):
    turned = [
        jnp.broadcast_to(ids_ref[:, k : k + 1].astype(F32), (TOK, TOK)).T.astype(jnp.int32)
        for k in range(TOP)
    ]
    hot = [row[:EXPERTS] == iota((EXPERTS, TOK), 0) for row in turned]
    table = (hot[0] | hot[1]).astype(F32).astype(BF16)
    before = (iota((TOK, TOK), 0) < iota((TOK, TOK), 1)).astype(F32).astype(BF16)
    earlier = dot(table, before)
    out = []
    for k in range(TOP):
        slot = jnp.sum(jnp.where(hot[k], earlier, 0.0), axis=0, keepdims=True)
        position = turned[k][:1] * CAP + slot.astype(jnp.int32)
        out.append(iota((SLOTS, TOK), 0) == position)
    return out


def patch_selects(ids_ref):
    hot = [ids_ref[:, k : k + 1] == iota((TOK, EXPERTS), 1) for k in range(TOP)]
    table = (hot[0] | hot[1]).astype(F32).astype(BF16)
    before = (iota((TOK, TOK), 1) < iota((TOK, TOK), 0)).astype(F32).astype(BF16)
    earlier = dot(before, table)
    out = []
    for k in range(TOP):
        slot = jnp.sum(jnp.where(hot[k], earlier, 0.0), axis=1, keepdims=True)
        position = ids_ref[:, k : k + 1] * CAP + slot.astype(jnp.int32)
        out.append(iota((TOK, SLOTS), 1) == position)
    return out


def as_bf16(mask):
    return mask.astype(F32).astype(BF16)


def depthwise(padded, taps_ref, flip, start, put):
    half = KSIZE // 2

    def chunk(c, _):
        lanes = pl.ds(pl.multiple_of(c * LANES, LANES), LANES)
        total = start(lanes)
        for col in range(KSIZE):
            begin = 8 + col - half
            shifted = padded[:, begin : begin + IMG_W, lanes]
            for row in range(KSIZE):
                tap = (KSIZE - 1 - row) * KSIZE + KSIZE - 1 - col if flip else row * KSIZE + col
                weight = taps_ref[tap : tap + 1, lanes]
                total = total + shifted[row : row + IMG_H] * weight[None]
        put(lanes, total)
        return 0

    lax.fori_loop(0, padded.shape[2] // LANES, chunk, 0)


def send_kernel(
    ids_ref,
    gates_ref,
    cot_ref,
    x_ref,
    taps_ref,
    bias_ref,
    gain_ref,
    shift_ref,
    sent_ref,
    xhat_ref,
    rstd_ref,
    padded,
    total,
):
    width = x_ref.shape[1]
    half = KSIZE // 2
    padded[...] = jnp.zeros_like(padded)
    padded[half : half + IMG_H, 8 : 8 + IMG_W, :] = (
        x_ref[...].astype(F32).reshape(IMG_H, IMG_W, width)
    )

    def start(lanes):
        return jnp.broadcast_to(bias_ref[:, lanes][None], (IMG_H, IMG_W, LANES))

    def put(lanes, value):
        total[:, lanes] = value.reshape(TOK, LANES)

    depthwise(padded, taps_ref, False, start, put)
    conv = total[...]
    mean = jnp.sum(conv, axis=1, keepdims=True) * (1.0 / width)
    centred = conv - mean
    spread = jnp.sum(centred * centred, axis=1, keepdims=True) * (1.0 / width)
    rstd = lax.rsqrt(spread + EPS)
    xhat = centred * rstd
    xhat_ref[...] = xhat
    rstd_ref[...] = jnp.broadcast_to(rstd, (TOK, LANES))
    normed = (xhat * gain_ref[...] + shift_ref[...]).astype(BF16)
    select = slot_selects(ids_ref)
    sent = dot(as_bf16(select[0] | select[1]), normed).astype(BF16)
    sent_ref[:, 0] = sent.reshape(EXPERTS, CAP, width)
    cot = cot_ref[...].astype(F32)
    first = (gates_ref[:, 0:1] * cot).astype(BF16)
    second = (gates_ref[:, 1:2] * cot).astype(BF16)
    sent = (dot(as_bf16(select[0]), first) + dot(as_bf16(select[1]), second)).astype(BF16)
    sent_ref[:, 1] = sent.reshape(EXPERTS, CAP, width)


def finish_kernel(
    ids_ref,
    gates_ref,
    back_ref,
    xhat_ref,
    rstd_ref,
    gain_ref,
    taps_ref,
    cot_ref,
    x_ref,
    mixed_ref,
    out_ref,
    padded,
):
    width = xhat_ref.shape[1]
    half = KSIZE // 2
    select = [as_bf16(mask) for mask in patch_selects(ids_ref)]
    rows = back_ref[:, 1].reshape(SLOTS, width)
    combined = gates_ref[:, 0:1] * dot(select[0], rows)
    combined = combined + gates_ref[:, 1:2] * dot(select[1], rows)
    mixed_ref[...] = (x_ref[...].astype(F32) + combined).astype(BF16)

    grad = dot(select[0] + select[1], back_ref[:, 0].reshape(SLOTS, width))
    grad = grad * gain_ref[...]
    xhat = xhat_ref[...]
    mean = jnp.sum(grad, axis=1, keepdims=True) * (1.0 / width)
    along = jnp.sum(grad * xhat, axis=1, keepdims=True) * (1.0 / width)
    grad = rstd_ref[:, 0:1] * (grad - mean - xhat * along)
    padded[...] = jnp.zeros_like(padded)
    padded[half : half + IMG_H, 8 : 8 + IMG_W, :] = grad.reshape(IMG_H, IMG_W, width)

    def start(lanes):
        return jnp.zeros((IMG_H, IMG_W, LANES), F32)

    def put(lanes, value):
        out_ref[:, lanes] = cot_ref[:, lanes].astype(F32) + value.reshape(TOK, LANES)

    depthwise(padded, taps_ref, True, start, put)


def contract_last(left, right):
    return lax.dot_general(left, right, (((1,), (1,)), ((), ())), preferred_element_type=F32)


def contract_first(left, right):
    return lax.dot_general(left, right, (((0,), (0,)), ((), ())), preferred_element_type=F32)


SQRT_2_OVER_PI = 0.7978845608028654


def expert_kernel(
    moved_ref,
    w_in_ref,
    w_out_ref,
    back_ref,
    terms_ref,
    hidden_s,
    gh_s,
    grad_total,
    out_total,
):
    step = pl.program_id(0)
    steps = pl.num_programs(0) // 2
    sources, _, count, width = moved_ref.shape
    flat = sources * count
    block = w_in_ref.shape[1]
    hid = hidden_s.shape[0] * block

    @pl.when(step < steps)
    def _():
        pre = dot(moved_ref[:, 0].reshape(flat, width), w_in_ref[...])
        raw = dot(moved_ref[:, 1].reshape(flat, width), w_out_ref[...])
        square = pre * pre
        t = jnp.tanh(SQRT_2_OVER_PI * (pre + 0.044715 * (pre * square)))
        cdf = 0.5 * (1.0 + t)
        hidden = (pre * cdf).astype(BF16)
        slope = cdf + pre * (0.5 * (1.0 - t * t)) * (
            SQRT_2_OVER_PI * (1.0 + (3 * 0.044715) * square)
        )
        gh = (raw * slope).astype(BF16)
        hidden_s[step] = hidden
        gh_s[step] = gh
        grad_part = contract_last(gh, w_in_ref[...])
        out_part = contract_last(hidden, w_out_ref[...])

        @pl.when(step == 0)
        def _():
            grad_total[...] = grad_part
            out_total[...] = out_part

        @pl.when(step > 0)
        def _():
            grad_total[...] += grad_part
            out_total[...] += out_part

    @pl.when(step == steps - 1)
    def _():
        back_ref[:, 0] = grad_total[...].astype(BF16).reshape(sources, count, width)
        back_ref[:, 1] = out_total[...].astype(BF16).reshape(sources, count, width)

    @pl.when(step >= steps)
    def _():
        lanes = pl.ds(pl.multiple_of((step - steps) * block, block), block)
        rows = moved_ref[:, 0, :, lanes].reshape(flat, block)
        grads = moved_ref[:, 1, :, lanes].reshape(flat, block)
        for j in range(hidden_s.shape[0]):
            at = slice(j * block, (j + 1) * block)
            terms_ref[:, at] = contract_first(rows, gh_s[j]).astype(BF16)
            at = slice(hid + j * block, hid + (j + 1) * block)
            terms_ref[:, at] = contract_first(grads, hidden_s[j]).astype(BF16)


def place_kernel(where_ref, *refs):
    pieces, out_ref = refs[:-1], refs[-1]
    for k, piece in enumerate(pieces):
        at = lax.rem(where_ref[0] + len(pieces) - k, len(pieces))
        out_ref[at] = piece[...]


def cut_kernel(where_ref, block_ref, *out_refs):
    parts = block_ref.shape[0]
    for k, out_ref in enumerate(out_refs):
        out_ref[...] = block_ref[lax.rem(where_ref[0] + k + 1, parts)]


def add_kernel(where_ref, block_ref, first_ref, second_ref, third_ref, in_ref, out_ref):
    hid = in_ref.shape[1]
    total = block_ref[where_ref[0]].astype(F32) + first_ref[...].astype(F32)
    total = total + second_ref[...].astype(F32) + third_ref[...].astype(F32)
    in_ref[...] = total[:, :hid]
    out_ref[...] = total[:, hid:]


def params(mib=16):
    return pltpu.CompilerParams(vmem_limit_bytes=mib * MIB)


def cost(flops, nbytes):
    return pl.CostEstimate(flops=int(flops), bytes_accessed=int(nbytes), transcendentals=0)


def shape(dims, dtype):
    return jax.ShapeDtypeStruct(dims, dtype)


def send(ids, gates, cot, x, taps, bias, gain, shift):
    width = x.shape[1]
    return pl.pallas_call(
        send_kernel,
        out_shape=(
            shape((EXPERTS, 2, CAP, width), BF16),
            shape((TOK, width), F32),
            shape((TOK, LANES), F32),
        ),
        in_specs=[VMEM] * 8,
        out_specs=[VMEM] * 3,
        scratch_shapes=[
            pltpu.VMEM((IMG_H + KSIZE - 1, IMG_W + 16, width), F32),
            pltpu.VMEM((TOK, width), F32),
        ],
        compiler_params=params(),
        cost_estimate=cost(100 * TOK * width * 20, 4 * SLOTS * width),
        name="send",
    )(ids, gates, cot, x, taps, bias.reshape(1, width), gain.reshape(1, width), shift.reshape(1, width))


def finish(ids, gates, back, xhat, rstd, gain, taps, cot, x):
    width = cot.shape[1]
    return pl.pallas_call(
        finish_kernel,
        out_shape=(shape((TOK, width), BF16), shape((TOK, width), F32)),
        in_specs=[VMEM] * 9,
        out_specs=[VMEM] * 2,
        scratch_shapes=[pltpu.VMEM((IMG_H + KSIZE - 1, IMG_W + 16, width), F32)],
        compiler_params=params(),
        cost_estimate=cost(100 * TOK * width * 20, 4 * SLOTS * width),
        name="finish",
    )(ids, gates, back, xhat, rstd, gain.reshape(1, width), taps, cot, x)


def expert(moved, w_in, w_out):
    sources, _, count, width = moved.shape
    flat = sources * count
    hid = w_in.shape[1]
    block = 256
    steps = hid // block
    whole = pl.BlockSpec(
        (sources, 2, count, width), lambda j: (0, 0, 0, 0), pipeline_mode=pl.Buffered(1)
    )
    weight = pl.BlockSpec((width, block), lambda j: (0, jnp.minimum(j, steps - 1)))
    return pl.pallas_call(
        expert_kernel,
        grid=(2 * steps,),
        out_shape=(
            pltpu.HBM((sources, 2, count, width), BF16),
            pltpu.HBM((width, 2 * hid), BF16),
        ),
        in_specs=[whole, weight, weight],
        out_specs=[
            pl.BlockSpec((sources, 2, count, width), lambda j: (0, 0, 0, 0)),
            pl.BlockSpec((block, 2 * hid), lambda j: (jnp.maximum(j - steps, 0), 0)),
        ],
        scratch_shapes=[
            pltpu.VMEM((steps, flat, block), BF16),
            pltpu.VMEM((steps, flat, block), BF16),
            pltpu.VMEM((flat, width), F32),
            pltpu.VMEM((flat, width), F32),
        ],
        compiler_params=params(32),
        cost_estimate=cost(12 * flat * width * hid, 12 * MIB),
        name="expert",
    )(moved, *(pltpu.with_memory_space_constraint(w, pltpu.HBM) for w in (w_in, w_out)))


SMEM = pl.BlockSpec(memory_space=pltpu.SMEM)


def place(where, pieces):
    dims = pieces[0].shape
    return pl.pallas_call(
        place_kernel,
        out_shape=shape((len(pieces),) + dims, BF16),
        in_specs=[SMEM] + [VMEM] * len(pieces),
        out_specs=VMEM,
        compiler_params=params(8),
        cost_estimate=cost(0, 4 * MIB),
        name="place",
    )(where, *pieces)


def exchange(rows, axes):
    return lax.all_to_all(rows, axes, split_axis=0, concat_axis=0, tiled=True)


def shifted(value, axis, k):
    n = lax.axis_size(axis)
    return lax.ppermute(value, axis, [(i, (i + k) % n) for i in range(n)])


def where_on(axis):
    return lax.axis_index(axis).astype(jnp.int32).reshape(1)


def gather_by(axis, piece):
    far, after, before = (shifted(piece, axis, k) for k in (2, 1, 3))
    return place(where_on(axis), [piece, after, far, before])


def sum_over_y(block):
    where = where_on("yh")
    parts, rows, columns = block.shape
    cuts = pl.pallas_call(
        cut_kernel,
        out_shape=[shape((rows, columns), BF16)] * (parts - 1),
        in_specs=[SMEM, VMEM],
        out_specs=[VMEM] * (parts - 1),
        compiler_params=params(8),
        cost_estimate=cost(0, 2 * MIB),
        name="cut",
    )(where, block)
    got = {k: shifted(cuts[k - 1], "yh", k) for k in (2, 1, 3)}
    hid = columns // 2
    return pl.pallas_call(
        add_kernel,
        out_shape=[shape((rows, hid), F32)] * 2,
        in_specs=[SMEM] + [VMEM] * parts,
        out_specs=[VMEM] * 2,
        compiler_params=params(8),
        cost_estimate=cost(0, 2 * MIB),
        name="add",
    )(where, block, got[1], got[2], got[3])


def local(
    patches,
    expert_ids,
    gate_weights,
    conv_weight,
    conv_bias,
    ln_gain,
    ln_shift,
    w_in,
    w_out,
    grad_mixed,
):
    hid = w_in.shape[2]
    dp = ("x", "yh")
    ep = ("z", "yl", "core")
    full_in = lax.all_gather(w_in, dp, axis=1, tiled=True)[0]
    sent, xhat, rstd = send(
        expert_ids,
        gate_weights,
        grad_mixed,
        patches,
        conv_weight,
        conv_bias,
        ln_gain,
        ln_shift,
    )
    moved = exchange(sent, ep)
    along_y = gather_by("yh", w_out[0])
    full_out = gather_by("x", along_y.reshape(-1, hid)).reshape(-1, hid)
    back, partial = expert(moved, full_in, full_out)
    over_x = lax.psum_scatter(partial, "x", scatter_dimension=0, tiled=True)
    returned = exchange(back, ep)
    grad_in, grad_out = sum_over_y(over_x.reshape(4, -1, 2 * hid))
    mixed, grad_input = finish(
        expert_ids,
        gate_weights,
        returned,
        xhat,
        rstd,
        ln_gain,
        conv_weight,
        grad_mixed,
        patches,
    )
    return (mixed, grad_input, grad_in[None], grad_out[None])


def solution(mesh):
    fine = Mesh(mesh.devices.reshape(4, 4, 8, 2, 2), ("x", "yh", "z", "yl", "core"))
    dp = ("x", "yh")
    ep = ("z", "yl", "core")
    rows = P(dp + ep, None)
    weight = P(ep, dp, None)
    return jax.shard_map(
        local,
        mesh=fine,
        in_specs=(rows, rows, rows, P(), P(), P(), P(), weight, weight, rows),
        out_specs=(rows, rows, weight, weight),
        check_vma=False,
    )
```

```python
import jax
import jax.numpy as jnp
from jax import lax
from jax.experimental import pallas as pl
from jax.experimental.pallas import tpu as pltpu
from jax.sharding import Mesh, PartitionSpec as P


KSIZE = 7
TOP = 2
IMG_W = 16
IMG_H = 8
EPS = 1e-06
EXPERTS = 32
CAP = 16
TOK = 128
SLOTS = EXPERTS * CAP
LANES = 128
F32 = jnp.float32
BF16 = jnp.bfloat16
MIB = 1 << 20

VMEM = pl.BlockSpec(memory_space=pltpu.VMEM)


def dot(a, b):
    return jnp.dot(a, b, preferred_element_type=F32)


def iota(shape, dim):
    return lax.broadcasted_iota(jnp.int32, shape, dim)


def slot_selects(ids_ref):
    turned = [
        jnp.broadcast_to(ids_ref[:, k : k + 1].astype(F32), (TOK, TOK)).T.astype(jnp.int32)
        for k in range(TOP)
    ]
    hot = [row[:EXPERTS] == iota((EXPERTS, TOK), 0) for row in turned]
    table = (hot[0] | hot[1]).astype(F32).astype(BF16)
    before = (iota((TOK, TOK), 0) < iota((TOK, TOK), 1)).astype(F32).astype(BF16)
    earlier = dot(table, before)
    out = []
    for k in range(TOP):
        slot = jnp.sum(jnp.where(hot[k], earlier, 0.0), axis=0, keepdims=True)
        position = turned[k][:1] * CAP + slot.astype(jnp.int32)
        out.append(iota((SLOTS, TOK), 0) == position)
    return out


def patch_selects(ids_ref):
    hot = [ids_ref[:, k : k + 1] == iota((TOK, EXPERTS), 1) for k in range(TOP)]
    table = (hot[0] | hot[1]).astype(F32).astype(BF16)
    before = (iota((TOK, TOK), 1) < iota((TOK, TOK), 0)).astype(F32).astype(BF16)
    earlier = dot(before, table)
    out = []
    for k in range(TOP):
        slot = jnp.sum(jnp.where(hot[k], earlier, 0.0), axis=1, keepdims=True)
        position = ids_ref[:, k : k + 1] * CAP + slot.astype(jnp.int32)
        out.append(iota((TOK, SLOTS), 1) == position)
    return out


def as_bf16(mask):
    return mask.astype(F32).astype(BF16)


def depthwise(padded, taps_ref, flip, start, put):
    half = KSIZE // 2

    def chunk(c, _):
        lanes = pl.ds(pl.multiple_of(c * LANES, LANES), LANES)
        total = start(lanes)
        for col in range(KSIZE):
            begin = 8 + col - half
            shifted = padded[:, begin : begin + IMG_W, lanes]
            for row in range(KSIZE):
                tap = (KSIZE - 1 - row) * KSIZE + KSIZE - 1 - col if flip else row * KSIZE + col
                weight = taps_ref[tap : tap + 1, lanes]
                total = total + shifted[row : row + IMG_H] * weight[None]
        put(lanes, total)
        return 0

    lax.fori_loop(0, padded.shape[2] // LANES, chunk, 0)


def send_kernel(
    ids_ref,
    gates_ref,
    cot_ref,
    x_ref,
    taps_ref,
    bias_ref,
    gain_ref,
    shift_ref,
    sent_ref,
    xhat_ref,
    rstd_ref,
    padded,
    total,
):
    width = x_ref.shape[1]
    half = KSIZE // 2
    padded[...] = jnp.zeros_like(padded)
    padded[half : half + IMG_H, 8 : 8 + IMG_W, :] = (
        x_ref[...].astype(F32).reshape(IMG_H, IMG_W, width)
    )

    def start(lanes):
        return jnp.broadcast_to(bias_ref[:, lanes][None], (IMG_H, IMG_W, LANES))

    def put(lanes, value):
        total[:, lanes] = value.reshape(TOK, LANES)

    depthwise(padded, taps_ref, False, start, put)
    conv = total[...]
    mean = jnp.sum(conv, axis=1, keepdims=True) * (1.0 / width)
    centred = conv - mean
    spread = jnp.sum(centred * centred, axis=1, keepdims=True) * (1.0 / width)
    rstd = lax.rsqrt(spread + EPS)
    xhat = centred * rstd
    xhat_ref[...] = xhat
    rstd_ref[...] = jnp.broadcast_to(rstd, (TOK, LANES))
    normed = (xhat * gain_ref[...] + shift_ref[...]).astype(BF16)
    select = slot_selects(ids_ref)
    sent = dot(as_bf16(select[0] | select[1]), normed).astype(BF16)
    sent_ref[:, 0] = sent.reshape(EXPERTS, CAP, width)
    cot = cot_ref[...].astype(F32)
    first = (gates_ref[:, 0:1] * cot).astype(BF16)
    second = (gates_ref[:, 1:2] * cot).astype(BF16)
    sent = (dot(as_bf16(select[0]), first) + dot(as_bf16(select[1]), second)).astype(BF16)
    sent_ref[:, 1] = sent.reshape(EXPERTS, CAP, width)


def finish_kernel(
    ids_ref,
    gates_ref,
    back_ref,
    xhat_ref,
    rstd_ref,
    gain_ref,
    taps_ref,
    cot_ref,
    x_ref,
    mixed_ref,
    out_ref,
    padded,
):
    width = xhat_ref.shape[1]
    half = KSIZE // 2
    select = [as_bf16(mask) for mask in patch_selects(ids_ref)]
    rows = back_ref[:, 1].reshape(SLOTS, width)
    combined = gates_ref[:, 0:1] * dot(select[0], rows)
    combined = combined + gates_ref[:, 1:2] * dot(select[1], rows)
    mixed_ref[...] = (x_ref[...].astype(F32) + combined).astype(BF16)

    grad = dot(select[0] + select[1], back_ref[:, 0].reshape(SLOTS, width))
    grad = grad * gain_ref[...]
    xhat = xhat_ref[...]
    mean = jnp.sum(grad, axis=1, keepdims=True) * (1.0 / width)
    along = jnp.sum(grad * xhat, axis=1, keepdims=True) * (1.0 / width)
    grad = rstd_ref[:, 0:1] * (grad - mean - xhat * along)
    padded[...] = jnp.zeros_like(padded)
    padded[half : half + IMG_H, 8 : 8 + IMG_W, :] = grad.reshape(IMG_H, IMG_W, width)

    def start(lanes):
        return jnp.zeros((IMG_H, IMG_W, LANES), F32)

    def put(lanes, value):
        out_ref[:, lanes] = cot_ref[:, lanes].astype(F32) + value.reshape(TOK, LANES)

    depthwise(padded, taps_ref, True, start, put)


def contract_last(left, right):
    return lax.dot_general(left, right, (((1,), (1,)), ((), ())), preferred_element_type=F32)


def contract_first(left, right):
    return lax.dot_general(left, right, (((0,), (0,)), ((), ())), preferred_element_type=F32)


SQRT_2_OVER_PI = 0.7978845608028654


def expert_kernel(
    moved_ref,
    w_in_ref,
    w_out_ref,
    back_ref,
    terms_ref,
    hidden_s,
    gh_s,
    grad_total,
    out_total,
):
    step = pl.program_id(0)
    steps = pl.num_programs(0) // 2
    sources, _, count, width = moved_ref.shape
    flat = sources * count
    block = w_in_ref.shape[1]
    hid = hidden_s.shape[0] * block

    @pl.when(step < steps)
    def _():
        pre = dot(moved_ref[:, 0].reshape(flat, width), w_in_ref[...])
        raw = dot(moved_ref[:, 1].reshape(flat, width), w_out_ref[...])
        square = pre * pre
        t = jnp.tanh(SQRT_2_OVER_PI * (pre + 0.044715 * (pre * square)))
        cdf = 0.5 * (1.0 + t)
        hidden = (pre * cdf).astype(BF16)
        slope = cdf + pre * (0.5 * (1.0 - t * t)) * (
            SQRT_2_OVER_PI * (1.0 + (3 * 0.044715) * square)
        )
        gh = (raw * slope).astype(BF16)
        hidden_s[step] = hidden
        gh_s[step] = gh
        grad_part = contract_last(gh, w_in_ref[...])
        out_part = contract_last(hidden, w_out_ref[...])

        @pl.when(step == 0)
        def _():
            grad_total[...] = grad_part
            out_total[...] = out_part

        @pl.when(step > 0)
        def _():
            grad_total[...] += grad_part
            out_total[...] += out_part

    @pl.when(step == steps - 1)
    def _():
        back_ref[:, 0] = grad_total[...].astype(BF16).reshape(sources, count, width)
        back_ref[:, 1] = out_total[...].astype(BF16).reshape(sources, count, width)

    @pl.when(step >= steps)
    def _():
        lanes = pl.ds(pl.multiple_of((step - steps) * block, block), block)
        rows = moved_ref[:, 0, :, lanes].reshape(flat, block)
        grads = moved_ref[:, 1, :, lanes].reshape(flat, block)
        for j in range(hidden_s.shape[0]):
            at = slice(j * block, (j + 1) * block)
            terms_ref[:, at] = contract_first(rows, gh_s[j]).astype(BF16)
            at = slice(hid + j * block, hid + (j + 1) * block)
            terms_ref[:, at] = contract_first(grads, hidden_s[j]).astype(BF16)


def place_kernel(where_ref, *refs):
    pieces, out_ref = refs[:-1], refs[-1]
    for k, piece in enumerate(pieces):
        at = lax.rem(where_ref[0] + len(pieces) - k, len(pieces))
        out_ref[at] = piece[...]


def params(mib=16):
    return pltpu.CompilerParams(vmem_limit_bytes=mib * MIB)


def cost(flops, nbytes):
    return pl.CostEstimate(flops=int(flops), bytes_accessed=int(nbytes), transcendentals=0)


def shape(dims, dtype):
    return jax.ShapeDtypeStruct(dims, dtype)


def send(ids, gates, cot, x, taps, bias, gain, shift):
    width = x.shape[1]
    return pl.pallas_call(
        send_kernel,
        out_shape=(
            shape((EXPERTS, 2, CAP, width), BF16),
            shape((TOK, width), F32),
            shape((TOK, LANES), F32),
        ),
        in_specs=[VMEM] * 8,
        out_specs=[VMEM] * 3,
        scratch_shapes=[
            pltpu.VMEM((IMG_H + KSIZE - 1, IMG_W + 16, width), F32),
            pltpu.VMEM((TOK, width), F32),
        ],
        compiler_params=params(),
        cost_estimate=cost(100 * TOK * width * 20, 4 * SLOTS * width),
        name="send",
    )(ids, gates, cot, x, taps, bias.reshape(1, width), gain.reshape(1, width), shift.reshape(1, width))


def finish(ids, gates, back, xhat, rstd, gain, taps, cot, x):
    width = cot.shape[1]
    return pl.pallas_call(
        finish_kernel,
        out_shape=(shape((TOK, width), BF16), shape((TOK, width), F32)),
        in_specs=[VMEM] * 9,
        out_specs=[VMEM] * 2,
        scratch_shapes=[pltpu.VMEM((IMG_H + KSIZE - 1, IMG_W + 16, width), F32)],
        compiler_params=params(),
        cost_estimate=cost(100 * TOK * width * 20, 4 * SLOTS * width),
        name="finish",
    )(ids, gates, back, xhat, rstd, gain.reshape(1, width), taps, cot, x)


def expert(moved, w_in, w_out):
    sources, _, count, width = moved.shape
    flat = sources * count
    hid = w_in.shape[1]
    block = 256
    steps = hid // block
    whole = pl.BlockSpec(
        (sources, 2, count, width), lambda j: (0, 0, 0, 0), pipeline_mode=pl.Buffered(1)
    )
    weight = pl.BlockSpec((width, block), lambda j: (0, jnp.minimum(j, steps - 1)))
    return pl.pallas_call(
        expert_kernel,
        grid=(2 * steps,),
        out_shape=(
            pltpu.HBM((sources, 2, count, width), BF16),
            pltpu.HBM((width, 2 * hid), BF16),
        ),
        in_specs=[whole, weight, weight],
        out_specs=[
            pl.BlockSpec((sources, 2, count, width), lambda j: (0, 0, 0, 0)),
            pl.BlockSpec((block, 2 * hid), lambda j: (jnp.maximum(j - steps, 0), 0)),
        ],
        scratch_shapes=[
            pltpu.VMEM((steps, flat, block), BF16),
            pltpu.VMEM((steps, flat, block), BF16),
            pltpu.VMEM((flat, width), F32),
            pltpu.VMEM((flat, width), F32),
        ],
        compiler_params=params(32),
        cost_estimate=cost(12 * flat * width * hid, 12 * MIB),
        name="expert",
    )(moved, *(pltpu.with_memory_space_constraint(w, pltpu.HBM) for w in (w_in, w_out)))


SMEM = pl.BlockSpec(memory_space=pltpu.SMEM)


def place(where, pieces):
    dims = pieces[0].shape
    return pl.pallas_call(
        place_kernel,
        out_shape=shape((len(pieces),) + dims, BF16),
        in_specs=[SMEM] + [VMEM] * len(pieces),
        out_specs=VMEM,
        compiler_params=params(8),
        cost_estimate=cost(0, 4 * MIB),
        name="place",
    )(where, *pieces)


def exchange(rows, axes):
    return lax.all_to_all(rows, axes, split_axis=0, concat_axis=0, tiled=True)


def shifted(value, axis, k):
    n = lax.axis_size(axis)
    return lax.ppermute(value, axis, [(i, (i + k) % n) for i in range(n)])


def where_on(axis):
    return lax.axis_index(axis).astype(jnp.int32).reshape(1)


def gather_by(axis, piece):
    far, after, before = (shifted(piece, axis, k) for k in (2, 1, 3))
    return place(where_on(axis), [piece, after, far, before])


def gather_y(piece):
    parts = lax.axis_size("yh")
    return exchange(jnp.broadcast_to(piece[None], (parts,) + piece.shape), "yh")


def local(
    patches,
    expert_ids,
    gate_weights,
    conv_weight,
    conv_bias,
    ln_gain,
    ln_shift,
    w_in,
    w_out,
    grad_mixed,
):
    hid = w_in.shape[2]
    dp = ("x", "yh")
    ep = ("z", "yl", "core")
    full_in = lax.all_gather(w_in, dp, axis=1, tiled=True)[0]
    sent, xhat, rstd = send(
        expert_ids,
        gate_weights,
        grad_mixed,
        patches,
        conv_weight,
        conv_bias,
        ln_gain,
        ln_shift,
    )
    moved = exchange(sent, ep)
    along_y = gather_y(w_out[0])
    full_out = gather_by("x", along_y.reshape(-1, hid)).reshape(-1, hid)
    back, partial = expert(moved, full_in, full_out)
    over_x = lax.psum_scatter(partial, "x", scatter_dimension=0, tiled=True)
    returned = exchange(back, ep)
    total = lax.psum_scatter(over_x, "yh", scatter_dimension=0, tiled=True).astype(F32)
    mixed, grad_input = finish(
        expert_ids,
        gate_weights,
        returned,
        xhat,
        rstd,
        ln_gain,
        conv_weight,
        grad_mixed,
        patches,
    )
    return (mixed, grad_input, total[:, :hid][None], total[:, hid:][None])


def solution(mesh):
    fine = Mesh(mesh.devices.reshape(4, 4, 8, 2, 2), ("x", "yh", "z", "yl", "core"))
    dp = ("x", "yh")
    ep = ("z", "yl", "core")
    rows = P(dp + ep, None)
    weight = P(ep, dp, None)
    return jax.shard_map(
        local,
        mesh=fine,
        in_specs=(rows, rows, rows, P(), P(), P(), P(), weight, weight, rows),
        out_specs=(rows, rows, weight, weight),
        check_vma=False,
    )
```

```python
import jax
import jax.numpy as jnp
from jax import lax
from jax.experimental import pallas as pl
from jax.experimental.pallas import tpu as pltpu
from jax.sharding import Mesh, PartitionSpec as P


KSIZE = 7
TOP = 2
IMG_W = 16
IMG_H = 8
EPS = 1e-06
EXPERTS = 32
CAP = 16
TOK = 128
SLOTS = EXPERTS * CAP
LANES = 128
F32 = jnp.float32
BF16 = jnp.bfloat16
MIB = 1 << 20

VMEM = pl.BlockSpec(memory_space=pltpu.VMEM)


def dot(a, b):
    return jnp.dot(a, b, preferred_element_type=F32)


def iota(shape, dim):
    return lax.broadcasted_iota(jnp.int32, shape, dim)


def slot_selects(ids_ref):
    turned = [
        jnp.broadcast_to(ids_ref[:, k : k + 1].astype(F32), (TOK, TOK)).T.astype(jnp.int32)
        for k in range(TOP)
    ]
    hot = [row[:EXPERTS] == iota((EXPERTS, TOK), 0) for row in turned]
    table = (hot[0] | hot[1]).astype(F32).astype(BF16)
    before = (iota((TOK, TOK), 0) < iota((TOK, TOK), 1)).astype(F32).astype(BF16)
    earlier = dot(table, before)
    out = []
    for k in range(TOP):
        slot = jnp.sum(jnp.where(hot[k], earlier, 0.0), axis=0, keepdims=True)
        position = turned[k][:1] * CAP + slot.astype(jnp.int32)
        out.append(iota((SLOTS, TOK), 0) == position)
    return out


def patch_selects(ids_ref):
    hot = [ids_ref[:, k : k + 1] == iota((TOK, EXPERTS), 1) for k in range(TOP)]
    table = (hot[0] | hot[1]).astype(F32).astype(BF16)
    before = (iota((TOK, TOK), 1) < iota((TOK, TOK), 0)).astype(F32).astype(BF16)
    earlier = dot(before, table)
    out = []
    for k in range(TOP):
        slot = jnp.sum(jnp.where(hot[k], earlier, 0.0), axis=1, keepdims=True)
        position = ids_ref[:, k : k + 1] * CAP + slot.astype(jnp.int32)
        out.append(iota((TOK, SLOTS), 1) == position)
    return out


def as_bf16(mask):
    return mask.astype(F32).astype(BF16)


def depthwise(padded, taps_ref, flip, start, put):
    half = KSIZE // 2

    def chunk(c, _):
        lanes = pl.ds(pl.multiple_of(c * LANES, LANES), LANES)
        total = start(lanes)
        for col in range(KSIZE):
            begin = 8 + col - half
            shifted = padded[:, begin : begin + IMG_W, lanes]
            for row in range(KSIZE):
                tap = (KSIZE - 1 - row) * KSIZE + KSIZE - 1 - col if flip else row * KSIZE + col
                weight = taps_ref[tap : tap + 1, lanes]
                total = total + shifted[row : row + IMG_H] * weight[None]
        put(lanes, total)
        return 0

    lax.fori_loop(0, padded.shape[2] // LANES, chunk, 0)


def send_kernel(
    ids_ref,
    gates_ref,
    cot_ref,
    x_ref,
    taps_ref,
    bias_ref,
    gain_ref,
    shift_ref,
    sent_ref,
    xhat_ref,
    rstd_ref,
    padded,
    total,
):
    width = x_ref.shape[1]
    half = KSIZE // 2
    padded[...] = jnp.zeros_like(padded)
    padded[half : half + IMG_H, 8 : 8 + IMG_W, :] = (
        x_ref[...].astype(F32).reshape(IMG_H, IMG_W, width)
    )

    def start(lanes):
        return jnp.broadcast_to(bias_ref[:, lanes][None], (IMG_H, IMG_W, LANES))

    def put(lanes, value):
        total[:, lanes] = value.reshape(TOK, LANES)

    depthwise(padded, taps_ref, False, start, put)
    conv = total[...]
    mean = jnp.sum(conv, axis=1, keepdims=True) * (1.0 / width)
    centred = conv - mean
    spread = jnp.sum(centred * centred, axis=1, keepdims=True) * (1.0 / width)
    rstd = lax.rsqrt(spread + EPS)
    xhat = centred * rstd
    xhat_ref[...] = xhat
    rstd_ref[...] = jnp.broadcast_to(rstd, (TOK, LANES))
    normed = (xhat * gain_ref[...] + shift_ref[...]).astype(BF16)
    select = slot_selects(ids_ref)
    sent = dot(as_bf16(select[0] | select[1]), normed).astype(BF16)
    sent_ref[:, 0] = sent.reshape(EXPERTS, CAP, width)
    cot = cot_ref[...].astype(F32)
    first = (gates_ref[:, 0:1] * cot).astype(BF16)
    second = (gates_ref[:, 1:2] * cot).astype(BF16)
    sent = (dot(as_bf16(select[0]), first) + dot(as_bf16(select[1]), second)).astype(BF16)
    sent_ref[:, 1] = sent.reshape(EXPERTS, CAP, width)


def finish_kernel(
    ids_ref,
    gates_ref,
    back_ref,
    xhat_ref,
    rstd_ref,
    gain_ref,
    taps_ref,
    cot_ref,
    x_ref,
    mixed_ref,
    out_ref,
    padded,
):
    width = xhat_ref.shape[1]
    half = KSIZE // 2
    select = [as_bf16(mask) for mask in patch_selects(ids_ref)]
    rows = back_ref[:, 1].reshape(SLOTS, width)
    combined = gates_ref[:, 0:1] * dot(select[0], rows)
    combined = combined + gates_ref[:, 1:2] * dot(select[1], rows)
    mixed_ref[...] = (x_ref[...].astype(F32) + combined).astype(BF16)

    grad = dot(select[0] + select[1], back_ref[:, 0].reshape(SLOTS, width))
    grad = grad * gain_ref[...]
    xhat = xhat_ref[...]
    mean = jnp.sum(grad, axis=1, keepdims=True) * (1.0 / width)
    along = jnp.sum(grad * xhat, axis=1, keepdims=True) * (1.0 / width)
    grad = rstd_ref[:, 0:1] * (grad - mean - xhat * along)
    padded[...] = jnp.zeros_like(padded)
    padded[half : half + IMG_H, 8 : 8 + IMG_W, :] = grad.reshape(IMG_H, IMG_W, width)

    def start(lanes):
        return jnp.zeros((IMG_H, IMG_W, LANES), F32)

    def put(lanes, value):
        out_ref[:, lanes] = cot_ref[:, lanes].astype(F32) + value.reshape(TOK, LANES)

    depthwise(padded, taps_ref, True, start, put)


def contract_last(left, right):
    return lax.dot_general(left, right, (((1,), (1,)), ((), ())), preferred_element_type=F32)


def contract_first(left, right):
    return lax.dot_general(left, right, (((0,), (0,)), ((), ())), preferred_element_type=F32)


SQRT_2_OVER_PI = 0.7978845608028654


def expert_kernel(moved_ref, w_in_ref, w_out_ref, terms_ref, hidden_ref, gh_ref):
    step = pl.program_id(0)
    steps = pl.num_programs(0) // 2
    sources, _, count, width = moved_ref.shape
    flat = sources * count
    block = w_in_ref.shape[1]
    hid = hidden_ref.shape[1]

    @pl.when(step < steps)
    def _():
        pre = dot(moved_ref[:, 0].reshape(flat, width), w_in_ref[...])
        raw = dot(moved_ref[:, 1].reshape(flat, width), w_out_ref[...])
        square = pre * pre
        t = jnp.tanh(SQRT_2_OVER_PI * (pre + 0.044715 * (pre * square)))
        cdf = 0.5 * (1.0 + t)
        slope = cdf + pre * (0.5 * (1.0 - t * t)) * (
            SQRT_2_OVER_PI * (1.0 + (3 * 0.044715) * square)
        )
        lanes = pl.ds(pl.multiple_of(step * block, block), block)
        hidden_ref[:, lanes] = (pre * cdf).astype(BF16)
        gh_ref[:, lanes] = (raw * slope).astype(BF16)

    @pl.when(step >= steps)
    def _():
        lanes = pl.ds(pl.multiple_of((step - steps) * block, block), block)
        rows = moved_ref[:, 0, :, lanes].reshape(flat, block)
        grads = moved_ref[:, 1, :, lanes].reshape(flat, block)
        terms_ref[:, :hid] = contract_first(rows, gh_ref[...]).astype(BF16)
        terms_ref[:, hid:] = contract_first(grads, hidden_ref[...]).astype(BF16)


def return_kernel(hidden_ref, gh_ref, w_in_ref, w_out_ref, back_ref):
    sources, _, count, block = back_ref.shape
    grad = contract_last(gh_ref[...], w_in_ref[...]).astype(BF16)
    back_ref[:, 0] = grad.reshape(sources, count, block)
    out = contract_last(hidden_ref[...], w_out_ref[...]).astype(BF16)
    back_ref[:, 1] = out.reshape(sources, count, block)


def place_kernel(where_ref, *refs):
    pieces, out_ref = refs[:-1], refs[-1]
    for k, piece in enumerate(pieces):
        at = lax.rem(where_ref[0] + len(pieces) - k, len(pieces))
        out_ref[at] = piece[...]


def params(mib=16):
    return pltpu.CompilerParams(vmem_limit_bytes=mib * MIB)


def cost(flops, nbytes):
    return pl.CostEstimate(flops=int(flops), bytes_accessed=int(nbytes), transcendentals=0)


def shape(dims, dtype):
    return jax.ShapeDtypeStruct(dims, dtype)


def send(ids, gates, cot, x, taps, bias, gain, shift):
    width = x.shape[1]
    return pl.pallas_call(
        send_kernel,
        out_shape=(
            shape((EXPERTS, 2, CAP, width), BF16),
            shape((TOK, width), F32),
            shape((TOK, LANES), F32),
        ),
        in_specs=[VMEM] * 8,
        out_specs=[VMEM] * 3,
        scratch_shapes=[
            pltpu.VMEM((IMG_H + KSIZE - 1, IMG_W + 16, width), F32),
            pltpu.VMEM((TOK, width), F32),
        ],
        compiler_params=params(),
        cost_estimate=cost(100 * TOK * width * 20, 4 * SLOTS * width),
        name="send",
    )(ids, gates, cot, x, taps, bias.reshape(1, width), gain.reshape(1, width), shift.reshape(1, width))


def finish(ids, gates, back, xhat, rstd, gain, taps, cot, x):
    width = cot.shape[1]
    return pl.pallas_call(
        finish_kernel,
        out_shape=(shape((TOK, width), BF16), shape((TOK, width), F32)),
        in_specs=[VMEM] * 9,
        out_specs=[VMEM] * 2,
        scratch_shapes=[pltpu.VMEM((IMG_H + KSIZE - 1, IMG_W + 16, width), F32)],
        compiler_params=params(),
        cost_estimate=cost(100 * TOK * width * 20, 4 * SLOTS * width),
        name="finish",
    )(ids, gates, back, xhat, rstd, gain.reshape(1, width), taps, cot, x)


def in_hbm(array):
    return pltpu.with_memory_space_constraint(array, pltpu.HBM)


def expert(moved, w_in, w_out):
    sources, _, count, width = moved.shape
    flat = sources * count
    hid = w_in.shape[1]
    block = 256
    steps = hid // block
    once = pl.Buffered(1)
    weight = pl.BlockSpec((width, block), lambda j: (0, jnp.minimum(j, steps - 1)))
    whole = pl.BlockSpec((flat, hid), lambda j: (0, 0))
    return pl.pallas_call(
        expert_kernel,
        grid=(2 * steps,),
        out_shape=(
            pltpu.HBM((width, 2 * hid), BF16),
            pltpu.HBM((flat, hid), BF16),
            pltpu.HBM((flat, hid), BF16),
        ),
        in_specs=[
            pl.BlockSpec(
                (sources, 2, count, width), lambda j: (0, 0, 0, 0), pipeline_mode=once
            ),
            weight,
            weight,
        ],
        out_specs=[
            pl.BlockSpec((block, 2 * hid), lambda j: (jnp.maximum(j - steps, 0), 0)),
            whole,
            whole,
        ],
        compiler_params=params(20),
        cost_estimate=cost(8 * flat * width * hid, 12 * MIB),
        name="expert",
    )(moved, in_hbm(w_in), in_hbm(w_out))


def return_rows(hidden, gh, w_in, w_out, sources):
    flat, hid = hidden.shape
    width = w_in.shape[0]
    block = 256
    count = flat // sources
    whole = pl.BlockSpec((flat, hid), lambda j: (0, 0), pipeline_mode=pl.Buffered(1))
    weight = pl.BlockSpec((block, hid), lambda j: (j, 0))
    return pl.pallas_call(
        return_kernel,
        grid=(width // block,),
        out_shape=pltpu.HBM((sources, 2, count, width), BF16),
        in_specs=[whole, whole, weight, weight],
        out_specs=pl.BlockSpec((sources, 2, count, block), lambda j: (0, 0, 0, j)),
        compiler_params=params(16),
        cost_estimate=cost(4 * flat * width * hid, 8 * MIB),
        name="return_rows",
    )(*(in_hbm(v) for v in (hidden, gh, w_in, w_out)))


SMEM = pl.BlockSpec(memory_space=pltpu.SMEM)


def place(where, pieces):
    dims = pieces[0].shape
    return pl.pallas_call(
        place_kernel,
        out_shape=shape((len(pieces),) + dims, BF16),
        in_specs=[SMEM] + [VMEM] * len(pieces),
        out_specs=VMEM,
        compiler_params=params(8),
        cost_estimate=cost(0, 4 * MIB),
        name="place",
    )(where, *pieces)


def exchange(rows, axes):
    return lax.all_to_all(rows, axes, split_axis=0, concat_axis=0, tiled=True)


def shifted(value, axis, k):
    n = lax.axis_size(axis)
    return lax.ppermute(value, axis, [(i, (i + k) % n) for i in range(n)])


def where_on(axis):
    return lax.axis_index(axis).astype(jnp.int32).reshape(1)


def gather_by(axis, piece):
    far, after, before = (shifted(piece, axis, k) for k in (2, 1, 3))
    return place(where_on(axis), [piece, after, far, before])


def gather_y(piece):
    parts = lax.axis_size("yh")
    return exchange(jnp.broadcast_to(piece[None], (parts,) + piece.shape), "yh")


def local(
    patches,
    expert_ids,
    gate_weights,
    conv_weight,
    conv_bias,
    ln_gain,
    ln_shift,
    w_in,
    w_out,
    grad_mixed,
):
    hid = w_in.shape[2]
    dp = ("x", "yh")
    ep = ("z", "yl", "core")
    full_in = lax.all_gather(w_in, dp, axis=1, tiled=True)[0]
    sent, xhat, rstd = send(
        expert_ids,
        gate_weights,
        grad_mixed,
        patches,
        conv_weight,
        conv_bias,
        ln_gain,
        ln_shift,
    )
    moved = exchange(sent, ep)
    along_y = gather_y(w_out[0])
    full_out = gather_by("x", along_y.reshape(-1, hid)).reshape(-1, hid)
    partial, hidden, gh = expert(moved, full_in, full_out)
    total = lax.psum_scatter(partial, dp, scatter_dimension=0, tiled=True).astype(F32)
    back = return_rows(hidden, gh, full_in, full_out, moved.shape[0])
    returned = exchange(back, ep)
    mixed, grad_input = finish(
        expert_ids,
        gate_weights,
        returned,
        xhat,
        rstd,
        ln_gain,
        conv_weight,
        grad_mixed,
        patches,
    )
    return (mixed, grad_input, total[:, :hid][None], total[:, hid:][None])


def solution(mesh):
    fine = Mesh(mesh.devices.reshape(4, 4, 8, 2, 2), ("x", "yh", "z", "yl", "core"))
    dp = ("x", "yh")
    ep = ("z", "yl", "core")
    rows = P(dp + ep, None)
    weight = P(ep, dp, None)
    return jax.shard_map(
        local,
        mesh=fine,
        in_specs=(rows, rows, rows, P(), P(), P(), P(), weight, weight, rows),
        out_specs=(rows, rows, weight, weight),
        check_vma=False,
    )
```

```python
import jax
import jax.numpy as jnp
from jax import lax
from jax.experimental import pallas as pl
from jax.experimental.pallas import tpu as pltpu
from jax.sharding import Mesh, PartitionSpec as P


KSIZE = 7
TOP = 2
IMG_W = 16
IMG_H = 8
EPS = 1e-06
EXPERTS = 32
CAP = 16
TOK = 128
SLOTS = EXPERTS * CAP
LANES = 128
F32 = jnp.float32
BF16 = jnp.bfloat16
MIB = 1 << 20

VMEM = pl.BlockSpec(memory_space=pltpu.VMEM)


def dot(a, b):
    return jnp.dot(a, b, preferred_element_type=F32)


def iota(shape, dim):
    return lax.broadcasted_iota(jnp.int32, shape, dim)


def slot_selects(ids_ref):
    turned = [
        jnp.broadcast_to(ids_ref[:, k : k + 1].astype(F32), (TOK, TOK)).T.astype(jnp.int32)
        for k in range(TOP)
    ]
    hot = [row[:EXPERTS] == iota((EXPERTS, TOK), 0) for row in turned]
    table = (hot[0] | hot[1]).astype(F32).astype(BF16)
    before = (iota((TOK, TOK), 0) < iota((TOK, TOK), 1)).astype(F32).astype(BF16)
    earlier = dot(table, before)
    out = []
    for k in range(TOP):
        slot = jnp.sum(jnp.where(hot[k], earlier, 0.0), axis=0, keepdims=True)
        position = turned[k][:1] * CAP + slot.astype(jnp.int32)
        out.append(iota((SLOTS, TOK), 0) == position)
    return out


def patch_selects(ids_ref):
    hot = [ids_ref[:, k : k + 1] == iota((TOK, EXPERTS), 1) for k in range(TOP)]
    table = (hot[0] | hot[1]).astype(F32).astype(BF16)
    before = (iota((TOK, TOK), 1) < iota((TOK, TOK), 0)).astype(F32).astype(BF16)
    earlier = dot(before, table)
    out = []
    for k in range(TOP):
        slot = jnp.sum(jnp.where(hot[k], earlier, 0.0), axis=1, keepdims=True)
        position = ids_ref[:, k : k + 1] * CAP + slot.astype(jnp.int32)
        out.append(iota((TOK, SLOTS), 1) == position)
    return out


def as_bf16(mask):
    return mask.astype(F32).astype(BF16)


def depthwise(padded, taps_ref, flip, start, put):
    half = KSIZE // 2

    def chunk(c, _):
        lanes = pl.ds(pl.multiple_of(c * LANES, LANES), LANES)
        total = start(lanes)
        for col in range(KSIZE):
            begin = 8 + col - half
            shifted = padded[:, begin : begin + IMG_W, lanes]
            for row in range(KSIZE):
                tap = (KSIZE - 1 - row) * KSIZE + KSIZE - 1 - col if flip else row * KSIZE + col
                weight = taps_ref[tap : tap + 1, lanes]
                total = total + shifted[row : row + IMG_H] * weight[None]
        put(lanes, total)
        return 0

    lax.fori_loop(0, padded.shape[2] // LANES, chunk, 0)


def send_kernel(
    ids_ref,
    gates_ref,
    cot_ref,
    x_ref,
    taps_ref,
    bias_ref,
    gain_ref,
    shift_ref,
    sent_ref,
    xhat_ref,
    rstd_ref,
    padded,
    total,
):
    width = x_ref.shape[1]
    half = KSIZE // 2
    padded[...] = jnp.zeros_like(padded)
    padded[half : half + IMG_H, 8 : 8 + IMG_W, :] = (
        x_ref[...].astype(F32).reshape(IMG_H, IMG_W, width)
    )

    def start(lanes):
        return jnp.broadcast_to(bias_ref[:, lanes][None], (IMG_H, IMG_W, LANES))

    def put(lanes, value):
        total[:, lanes] = value.reshape(TOK, LANES)

    depthwise(padded, taps_ref, False, start, put)
    conv = total[...]
    mean = jnp.sum(conv, axis=1, keepdims=True) * (1.0 / width)
    centred = conv - mean
    spread = jnp.sum(centred * centred, axis=1, keepdims=True) * (1.0 / width)
    rstd = lax.rsqrt(spread + EPS)
    xhat = centred * rstd
    xhat_ref[...] = xhat
    rstd_ref[...] = jnp.broadcast_to(rstd, (TOK, LANES))
    normed = (xhat * gain_ref[...] + shift_ref[...]).astype(BF16)
    select = slot_selects(ids_ref)
    sent = dot(as_bf16(select[0] | select[1]), normed).astype(BF16)
    sent_ref[:, 0] = sent.reshape(EXPERTS, CAP, width)
    cot = cot_ref[...].astype(F32)
    first = (gates_ref[:, 0:1] * cot).astype(BF16)
    second = (gates_ref[:, 1:2] * cot).astype(BF16)
    sent = (dot(as_bf16(select[0]), first) + dot(as_bf16(select[1]), second)).astype(BF16)
    sent_ref[:, 1] = sent.reshape(EXPERTS, CAP, width)


def finish_kernel(
    ids_ref,
    gates_ref,
    back_ref,
    xhat_ref,
    rstd_ref,
    gain_ref,
    taps_ref,
    cot_ref,
    x_ref,
    mixed_ref,
    out_ref,
    padded,
):
    width = xhat_ref.shape[1]
    half = KSIZE // 2
    select = [as_bf16(mask) for mask in patch_selects(ids_ref)]
    rows = back_ref[:, 1].reshape(SLOTS, width)
    combined = gates_ref[:, 0:1] * dot(select[0], rows)
    combined = combined + gates_ref[:, 1:2] * dot(select[1], rows)
    mixed_ref[...] = (x_ref[...].astype(F32) + combined).astype(BF16)

    grad = dot(select[0] + select[1], back_ref[:, 0].reshape(SLOTS, width))
    grad = grad * gain_ref[...]
    xhat = xhat_ref[...]
    mean = jnp.sum(grad, axis=1, keepdims=True) * (1.0 / width)
    along = jnp.sum(grad * xhat, axis=1, keepdims=True) * (1.0 / width)
    grad = rstd_ref[:, 0:1] * (grad - mean - xhat * along)
    padded[...] = jnp.zeros_like(padded)
    padded[half : half + IMG_H, 8 : 8 + IMG_W, :] = grad.reshape(IMG_H, IMG_W, width)

    def start(lanes):
        return jnp.zeros((IMG_H, IMG_W, LANES), F32)

    def put(lanes, value):
        out_ref[:, lanes] = cot_ref[:, lanes].astype(F32) + value.reshape(TOK, LANES)

    depthwise(padded, taps_ref, True, start, put)


def contract_last(left, right):
    return lax.dot_general(left, right, (((1,), (1,)), ((), ())), preferred_element_type=F32)


def contract_first(left, right):
    return lax.dot_general(left, right, (((0,), (0,)), ((), ())), preferred_element_type=F32)


SQRT_2_OVER_PI = 0.7978845608028654


def expert_kernel(
    where_ref,
    moved_ref,
    w_in_ref,
    w_out_ref,
    term_ref,
    own_ref,
    after_ref,
    far_ref,
    before_ref,
    hidden_ref,
    gh_ref,
    hidden_s,
    gh_s,
):
    step = pl.program_id(0)
    sources, _, count, width = moved_ref.shape
    flat = sources * count
    block = w_in_ref.shape[1]
    part = term_ref.shape[0]
    steps = hidden_s.shape[1] // block

    @pl.when(step < steps)
    def _():
        pre = dot(moved_ref[:, 0].reshape(flat, width), w_in_ref[...])
        raw = dot(moved_ref[:, 1].reshape(flat, width), w_out_ref[...])
        square = pre * pre
        t = jnp.tanh(SQRT_2_OVER_PI * (pre + 0.044715 * (pre * square)))
        cdf = 0.5 * (1.0 + t)
        slope = cdf + pre * (0.5 * (1.0 - t * t)) * (
            SQRT_2_OVER_PI * (1.0 + (3 * 0.044715) * square)
        )
        lanes = pl.ds(pl.multiple_of(step * block, block), block)
        hidden = (pre * cdf).astype(BF16)
        gh = (raw * slope).astype(BF16)
        hidden_s[:, lanes] = hidden
        gh_s[:, lanes] = gh
        hidden_ref[...] = hidden
        gh_ref[...] = gh

    @pl.when(step >= steps)
    def _():
        owner = lax.rem(where_ref[0] + step - steps, width // part)
        lanes = pl.ds(pl.multiple_of(owner * part, part), part)
        rows = moved_ref[:, 0, :, lanes].reshape(flat, part)
        grads = moved_ref[:, 1, :, lanes].reshape(flat, part)
        term_ref[...] = contract_first(rows, gh_s[...]).astype(BF16)
        value = contract_first(grads, hidden_s[...]).astype(BF16)
        for k, out_ref in enumerate((own_ref, after_ref, far_ref, before_ref)):

            @pl.when(step == steps + k)
            def _(out_ref=out_ref):
                out_ref[...] = value


def return_kernel(hidden_ref, gh_ref, w_in_ref, w_out_ref, back_ref):
    sources, _, count, block = back_ref.shape
    grad = contract_last(gh_ref[...], w_in_ref[...]).astype(BF16)
    back_ref[:, 0] = grad.reshape(sources, count, block)
    out = contract_last(hidden_ref[...], w_out_ref[...]).astype(BF16)
    back_ref[:, 1] = out.reshape(sources, count, block)


def join_kernel(first_ref, own_ref, after_ref, far_ref, before_ref, out_ref):
    half = first_ref.shape[1]
    out_ref[:, :half] = first_ref[...]
    total = own_ref[...].astype(F32) + after_ref[...].astype(F32)
    total = total + far_ref[...].astype(F32) + before_ref[...].astype(F32)
    out_ref[:, half:] = total.astype(BF16)


def place_kernel(where_ref, *refs):
    pieces, out_ref = refs[:-1], refs[-1]
    for k, piece in enumerate(pieces):
        at = lax.rem(where_ref[0] + len(pieces) - k, len(pieces))
        out_ref[at] = piece[...]


def params(mib=16):
    return pltpu.CompilerParams(vmem_limit_bytes=mib * MIB)


def cost(flops, nbytes):
    return pl.CostEstimate(flops=int(flops), bytes_accessed=int(nbytes), transcendentals=0)


def shape(dims, dtype):
    return jax.ShapeDtypeStruct(dims, dtype)


def send(ids, gates, cot, x, taps, bias, gain, shift):
    width = x.shape[1]
    return pl.pallas_call(
        send_kernel,
        out_shape=(
            shape((EXPERTS, 2, CAP, width), BF16),
            shape((TOK, width), F32),
            shape((TOK, LANES), F32),
        ),
        in_specs=[VMEM] * 8,
        out_specs=[VMEM] * 3,
        scratch_shapes=[
            pltpu.VMEM((IMG_H + KSIZE - 1, IMG_W + 16, width), F32),
            pltpu.VMEM((TOK, width), F32),
        ],
        compiler_params=params(),
        cost_estimate=cost(100 * TOK * width * 20, 4 * SLOTS * width),
        name="send",
    )(ids, gates, cot, x, taps, bias.reshape(1, width), gain.reshape(1, width), shift.reshape(1, width))


def finish(ids, gates, back, xhat, rstd, gain, taps, cot, x):
    width = cot.shape[1]
    return pl.pallas_call(
        finish_kernel,
        out_shape=(shape((TOK, width), BF16), shape((TOK, width), F32)),
        in_specs=[VMEM] * 9,
        out_specs=[VMEM] * 2,
        scratch_shapes=[pltpu.VMEM((IMG_H + KSIZE - 1, IMG_W + 16, width), F32)],
        compiler_params=params(),
        cost_estimate=cost(100 * TOK * width * 20, 4 * SLOTS * width),
        name="finish",
    )(ids, gates, back, xhat, rstd, gain.reshape(1, width), taps, cot, x)


def in_hbm(array):
    return pltpu.with_memory_space_constraint(array, pltpu.HBM)


def expert(where, moved, w_in, w_out):
    sources, _, count, width = moved.shape
    flat = sources * count
    hid = w_in.shape[1]
    block = 512
    steps = hid // block
    part = width // 4
    weight = pl.BlockSpec((width, block), lambda j, w: (0, jnp.minimum(j, steps - 1)))
    piece = pl.BlockSpec((part, hid), lambda j, w: (0, 0))
    hidden = pl.BlockSpec((flat, block), lambda j, w: (0, jnp.minimum(j, steps - 1)))
    grid_spec = pltpu.PrefetchScalarGridSpec(
        num_scalar_prefetch=1,
        grid=(steps + 4,),
        in_specs=[pl.BlockSpec(memory_space=pltpu.VMEM), weight, weight],
        out_specs=[
            pl.BlockSpec(
                (part, hid), lambda j, w: (lax.rem(w[0] + jnp.maximum(j - steps, 0), 4), 0)
            ),
            piece,
            piece,
            piece,
            piece,
            hidden,
            hidden,
        ],
        scratch_shapes=[pltpu.VMEM((flat, hid), BF16)] * 2,
    )
    return pl.pallas_call(
        expert_kernel,
        grid_spec=grid_spec,
        out_shape=(
            pltpu.HBM((width, hid), BF16),
            *(pltpu.HBM((part, hid), BF16) for _ in range(4)),
            pltpu.HBM((flat, hid), BF16),
            pltpu.HBM((flat, hid), BF16),
        ),
        compiler_params=params(30),
        cost_estimate=cost(8 * flat * width * hid, 12 * MIB),
        name="expert",
    )(where, moved, in_hbm(w_in), in_hbm(w_out))


def join(first, pieces):
    rows, half = first.shape
    return pl.pallas_call(
        join_kernel,
        out_shape=pltpu.HBM((rows, 2 * half), BF16),
        grid=(2,),
        in_specs=[pl.BlockSpec((rows // 2, half), lambda i: (i, 0))] * 5,
        out_specs=pl.BlockSpec((rows // 2, 2 * half), lambda i: (i, 0)),
        compiler_params=params(8),
        cost_estimate=cost(0, 3 * MIB),
        name="join",
    )(*(in_hbm(v) for v in (first, *pieces)))


def return_rows(hidden, gh, w_in, w_out, sources):
    flat, hid = hidden.shape
    width = w_in.shape[0]
    block = 256
    count = flat // sources
    whole = pl.BlockSpec((flat, hid), lambda j: (0, 0), pipeline_mode=pl.Buffered(1))
    weight = pl.BlockSpec((block, hid), lambda j: (j, 0))
    return pl.pallas_call(
        return_kernel,
        grid=(width // block,),
        out_shape=pltpu.HBM((sources, 2, count, width), BF16),
        in_specs=[whole, whole, weight, weight],
        out_specs=pl.BlockSpec((sources, 2, count, block), lambda j: (0, 0, 0, j)),
        compiler_params=params(16),
        cost_estimate=cost(4 * flat * width * hid, 8 * MIB),
        name="return_rows",
    )(*(in_hbm(v) for v in (hidden, gh, w_in, w_out)))


SMEM = pl.BlockSpec(memory_space=pltpu.SMEM)


def place(where, pieces):
    dims = pieces[0].shape
    return pl.pallas_call(
        place_kernel,
        out_shape=shape((len(pieces),) + dims, BF16),
        in_specs=[SMEM] + [VMEM] * len(pieces),
        out_specs=VMEM,
        compiler_params=params(8),
        cost_estimate=cost(0, 4 * MIB),
        name="place",
    )(where, *pieces)


def exchange(rows, axes):
    return lax.all_to_all(rows, axes, split_axis=0, concat_axis=0, tiled=True)


def shifted(value, axis, k):
    n = lax.axis_size(axis)
    return lax.ppermute(value, axis, [(i, (i + k) % n) for i in range(n)])


def where_on(axis):
    return lax.axis_index(axis).astype(jnp.int32).reshape(1)


def gather_by(axis, piece):
    far, after, before = (shifted(piece, axis, k) for k in (2, 1, 3))
    return place(where_on(axis), [piece, after, far, before])


def gather_y(piece):
    parts = lax.axis_size("yh")
    return exchange(jnp.broadcast_to(piece[None], (parts,) + piece.shape), "yh")


def local(
    patches,
    expert_ids,
    gate_weights,
    conv_weight,
    conv_bias,
    ln_gain,
    ln_shift,
    w_in,
    w_out,
    grad_mixed,
):
    hid = w_in.shape[2]
    dp = ("x", "yh")
    ep = ("z", "yl", "core")
    full_in = lax.all_gather(w_in, dp, axis=1, tiled=True)[0]
    sent, xhat, rstd = send(
        expert_ids,
        gate_weights,
        grad_mixed,
        patches,
        conv_weight,
        conv_bias,
        ln_gain,
        ln_shift,
    )
    moved = exchange(sent, ep)
    along_y = gather_y(w_out[0])
    full_out = gather_by("x", along_y.reshape(-1, hid)).reshape(-1, hid)
    term, own, *others, hidden, gh = expert(where_on("x"), moved, full_in, full_out)
    over_x = lax.psum_scatter(term, "x", scatter_dimension=0, tiled=True)
    back = return_rows(hidden, gh, full_in, full_out, moved.shape[0])
    returned = exchange(back, ep)
    got = {k: shifted(others[k - 1], "x", k) for k in (2, 1, 3)}
    joined = join(over_x, [own, got[1], got[2], got[3]])
    total = lax.psum_scatter(joined, "yh", scatter_dimension=0, tiled=True)
    grad_in = total[:, :hid].astype(F32)[None]
    grad_out = total[:, hid:].astype(F32)[None]
    mixed, grad_input = finish(
        expert_ids,
        gate_weights,
        returned,
        xhat,
        rstd,
        ln_gain,
        conv_weight,
        grad_mixed,
        patches,
    )
    return (mixed, grad_input, grad_in, grad_out)


def solution(mesh):
    fine = Mesh(mesh.devices.reshape(4, 4, 8, 2, 2), ("x", "yh", "z", "yl", "core"))
    dp = ("x", "yh")
    ep = ("z", "yl", "core")
    rows = P(dp + ep, None)
    weight = P(ep, dp, None)
    return jax.shard_map(
        local,
        mesh=fine,
        in_specs=(rows, rows, rows, P(), P(), P(), P(), weight, weight, rows),
        out_specs=(rows, rows, weight, weight),
        check_vma=False,
    )
```

```python
import jax
import jax.numpy as jnp
from jax import lax
from jax.experimental import pallas as pl
from jax.experimental.pallas import tpu as pltpu
from jax.sharding import Mesh, PartitionSpec as P


KSIZE = 7
TOP = 2
IMG_W = 16
IMG_H = 8
EPS = 1e-06
EXPERTS = 32
CAP = 16
TOK = 128
SLOTS = EXPERTS * CAP
LANES = 128
F32 = jnp.float32
BF16 = jnp.bfloat16
MIB = 1 << 20

VMEM = pl.BlockSpec(memory_space=pltpu.VMEM)


def dot(a, b):
    return jnp.dot(a, b, preferred_element_type=F32)


def iota(shape, dim):
    return lax.broadcasted_iota(jnp.int32, shape, dim)


def slot_selects(ids_ref):
    turned = [
        jnp.broadcast_to(ids_ref[:, k : k + 1].astype(F32), (TOK, TOK)).T.astype(jnp.int32)
        for k in range(TOP)
    ]
    hot = [row[:EXPERTS] == iota((EXPERTS, TOK), 0) for row in turned]
    table = (hot[0] | hot[1]).astype(F32).astype(BF16)
    before = (iota((TOK, TOK), 0) < iota((TOK, TOK), 1)).astype(F32).astype(BF16)
    earlier = dot(table, before)
    out = []
    for k in range(TOP):
        slot = jnp.sum(jnp.where(hot[k], earlier, 0.0), axis=0, keepdims=True)
        position = turned[k][:1] * CAP + slot.astype(jnp.int32)
        out.append(iota((SLOTS, TOK), 0) == position)
    return out


def patch_selects(ids_ref):
    hot = [ids_ref[:, k : k + 1] == iota((TOK, EXPERTS), 1) for k in range(TOP)]
    table = (hot[0] | hot[1]).astype(F32).astype(BF16)
    before = (iota((TOK, TOK), 1) < iota((TOK, TOK), 0)).astype(F32).astype(BF16)
    earlier = dot(before, table)
    out = []
    for k in range(TOP):
        slot = jnp.sum(jnp.where(hot[k], earlier, 0.0), axis=1, keepdims=True)
        position = ids_ref[:, k : k + 1] * CAP + slot.astype(jnp.int32)
        out.append(iota((TOK, SLOTS), 1) == position)
    return out


def as_bf16(mask):
    return mask.astype(F32).astype(BF16)


def depthwise(padded, taps_ref, flip, start, put):
    half = KSIZE // 2

    def chunk(c, _):
        lanes = pl.ds(pl.multiple_of(c * LANES, LANES), LANES)
        total = start(lanes)
        for col in range(KSIZE):
            begin = 8 + col - half
            shifted = padded[:, begin : begin + IMG_W, lanes]
            for row in range(KSIZE):
                tap = (KSIZE - 1 - row) * KSIZE + KSIZE - 1 - col if flip else row * KSIZE + col
                weight = taps_ref[tap : tap + 1, lanes]
                total = total + shifted[row : row + IMG_H] * weight[None]
        put(lanes, total)
        return 0

    lax.fori_loop(0, padded.shape[2] // LANES, chunk, 0)


def send_kernel(
    ids_ref,
    gates_ref,
    cot_ref,
    x_ref,
    taps_ref,
    bias_ref,
    gain_ref,
    shift_ref,
    sent_ref,
    xhat_ref,
    rstd_ref,
    padded,
    total,
):
    width = x_ref.shape[1]
    half = KSIZE // 2
    padded[...] = jnp.zeros_like(padded)
    padded[half : half + IMG_H, 8 : 8 + IMG_W, :] = (
        x_ref[...].astype(F32).reshape(IMG_H, IMG_W, width)
    )

    def start(lanes):
        return jnp.broadcast_to(bias_ref[:, lanes][None], (IMG_H, IMG_W, LANES))

    def put(lanes, value):
        total[:, lanes] = value.reshape(TOK, LANES)

    depthwise(padded, taps_ref, False, start, put)
    conv = total[...]
    mean = jnp.sum(conv, axis=1, keepdims=True) * (1.0 / width)
    centred = conv - mean
    spread = jnp.sum(centred * centred, axis=1, keepdims=True) * (1.0 / width)
    rstd = lax.rsqrt(spread + EPS)
    xhat = centred * rstd
    xhat_ref[...] = xhat
    rstd_ref[...] = jnp.broadcast_to(rstd, (TOK, LANES))
    normed = (xhat * gain_ref[...] + shift_ref[...]).astype(BF16)
    select = slot_selects(ids_ref)
    sent = dot(as_bf16(select[0] | select[1]), normed).astype(BF16)
    sent_ref[:, 0] = sent.reshape(EXPERTS, CAP, width)
    cot = cot_ref[...].astype(F32)
    first = (gates_ref[:, 0:1] * cot).astype(BF16)
    second = (gates_ref[:, 1:2] * cot).astype(BF16)
    sent = (dot(as_bf16(select[0]), first) + dot(as_bf16(select[1]), second)).astype(BF16)
    sent_ref[:, 1] = sent.reshape(EXPERTS, CAP, width)


def finish_kernel(
    ids_ref,
    gates_ref,
    back_ref,
    xhat_ref,
    rstd_ref,
    gain_ref,
    taps_ref,
    cot_ref,
    x_ref,
    mixed_ref,
    out_ref,
    padded,
):
    width = xhat_ref.shape[1]
    half = KSIZE // 2
    select = [as_bf16(mask) for mask in patch_selects(ids_ref)]
    rows = back_ref[:, 1].reshape(SLOTS, width)
    combined = gates_ref[:, 0:1] * dot(select[0], rows)
    combined = combined + gates_ref[:, 1:2] * dot(select[1], rows)
    mixed_ref[...] = (x_ref[...].astype(F32) + combined).astype(BF16)

    grad = dot(select[0] + select[1], back_ref[:, 0].reshape(SLOTS, width))
    grad = grad * gain_ref[...]
    xhat = xhat_ref[...]
    mean = jnp.sum(grad, axis=1, keepdims=True) * (1.0 / width)
    along = jnp.sum(grad * xhat, axis=1, keepdims=True) * (1.0 / width)
    grad = rstd_ref[:, 0:1] * (grad - mean - xhat * along)
    padded[...] = jnp.zeros_like(padded)
    padded[half : half + IMG_H, 8 : 8 + IMG_W, :] = grad.reshape(IMG_H, IMG_W, width)

    def start(lanes):
        return jnp.zeros((IMG_H, IMG_W, LANES), F32)

    def put(lanes, value):
        out_ref[:, lanes] = cot_ref[:, lanes].astype(F32) + value.reshape(TOK, LANES)

    depthwise(padded, taps_ref, True, start, put)


def contract_last(left, right):
    return lax.dot_general(left, right, (((1,), (1,)), ((), ())), preferred_element_type=F32)


def contract_first(left, right):
    return lax.dot_general(left, right, (((0,), (0,)), ((), ())), preferred_element_type=F32)


SQRT_2_OVER_PI = 0.7978845608028654


def expert_kernel(
    moved_ref,
    w_in_ref,
    w_out_ref,
    terms_ref,
    hidden_ref,
    gh_ref,
    hidden_s,
    gh_s,
):
    step = pl.program_id(0)
    sources, _, count, width = moved_ref.shape
    flat = sources * count
    block = w_in_ref.shape[1]
    part = terms_ref.shape[0]
    steps = hidden_s.shape[1] // block

    @pl.when(step < steps)
    def _():
        pre = dot(moved_ref[:, 0].reshape(flat, width), w_in_ref[...])
        raw = dot(moved_ref[:, 1].reshape(flat, width), w_out_ref[...])
        square = pre * pre
        t = jnp.tanh(SQRT_2_OVER_PI * (pre + 0.044715 * (pre * square)))
        cdf = 0.5 * (1.0 + t)
        slope = cdf + pre * (0.5 * (1.0 - t * t)) * (
            SQRT_2_OVER_PI * (1.0 + (3 * 0.044715) * square)
        )
        lanes = pl.ds(pl.multiple_of(step * block, block), block)
        hidden = (pre * cdf).astype(BF16)
        gh = (raw * slope).astype(BF16)
        hidden_s[:, lanes] = hidden
        gh_s[:, lanes] = gh
        hidden_ref[...] = hidden
        gh_ref[...] = gh

    @pl.when(step >= steps)
    def _():
        lanes = pl.ds(pl.multiple_of((step - steps) * part, part), part)
        rows = moved_ref[:, 0, :, lanes].reshape(flat, part)
        grads = moved_ref[:, 1, :, lanes].reshape(flat, part)
        hid = hidden_s.shape[1]
        terms_ref[:, :hid] = contract_first(rows, gh_s[...]).astype(BF16)
        terms_ref[:, hid:] = contract_first(grads, hidden_s[...]).astype(BF16)


def return_kernel(hidden_ref, gh_ref, w_in_ref, w_out_ref, back_ref):
    sources, _, count, block = back_ref.shape
    grad = contract_last(gh_ref[...], w_in_ref[...]).astype(BF16)
    back_ref[:, 0] = grad.reshape(sources, count, block)
    out = contract_last(hidden_ref[...], w_out_ref[...]).astype(BF16)
    back_ref[:, 1] = out.reshape(sources, count, block)


def widen_kernel(sum_ref, in_ref, out_ref):
    hid = in_ref.shape[1]
    in_ref[...] = sum_ref[:, :hid].astype(F32)
    out_ref[...] = sum_ref[:, hid:].astype(F32)


def place_kernel(where_ref, *refs):
    pieces, out_ref = refs[:-1], refs[-1]
    for k, piece in enumerate(pieces):
        at = lax.rem(where_ref[0] + len(pieces) - k, len(pieces))
        out_ref[at] = piece[...]


def params(mib=16):
    return pltpu.CompilerParams(vmem_limit_bytes=mib * MIB)


def cost(flops, nbytes):
    return pl.CostEstimate(flops=int(flops), bytes_accessed=int(nbytes), transcendentals=0)


def shape(dims, dtype):
    return jax.ShapeDtypeStruct(dims, dtype)


def in_hbm(array):
    return pltpu.with_memory_space_constraint(array, pltpu.HBM)


def all_of(dims):
    return pl.BlockSpec(dims, lambda i: (0,) * len(dims))


def send(ids, gates, cot, x, taps, bias, gain, shift):
    width = x.shape[1]
    rows = [bias.reshape(1, width), gain.reshape(1, width), shift.reshape(1, width)]
    outs = [((EXPERTS, 2, CAP, width), BF16), ((TOK, width), F32), ((TOK, LANES), F32)]
    wide = [in_hbm(v) for v in (cot, x, taps)]
    return pl.pallas_call(
        send_kernel,
        grid=(1,),
        out_shape=tuple(pltpu.HBM(*out) for out in outs),
        in_specs=[VMEM] * 2 + [all_of(v.shape) for v in wide] + [VMEM] * 3,
        out_specs=[all_of(dims) for dims, _ in outs],
        scratch_shapes=[
            pltpu.VMEM((IMG_H + KSIZE - 1, IMG_W + 16, width), F32),
            pltpu.VMEM((TOK, width), F32),
        ],
        compiler_params=params(20),
        cost_estimate=cost(100 * TOK * width * 20, 4 * SLOTS * width),
        name="send",
    )(ids, gates, *wide, *rows)


def finish(ids, gates, back, xhat, rstd, gain, taps, cot, x):
    width = cot.shape[1]
    return pl.pallas_call(
        finish_kernel,
        out_shape=(shape((TOK, width), BF16), shape((TOK, width), F32)),
        in_specs=[VMEM] * 9,
        out_specs=[VMEM] * 2,
        scratch_shapes=[pltpu.VMEM((IMG_H + KSIZE - 1, IMG_W + 16, width), F32)],
        compiler_params=params(),
        cost_estimate=cost(100 * TOK * width * 20, 4 * SLOTS * width),
        name="finish",
    )(ids, gates, back, xhat, rstd, gain.reshape(1, width), taps, cot, x)


def expert(moved, w_in, w_out):
    sources, _, count, width = moved.shape
    flat = sources * count
    hid = w_in.shape[1]
    block = 512
    part = 256
    steps = hid // block
    weight = pl.BlockSpec((width, block), lambda j: (0, jnp.minimum(j, steps - 1)))
    hidden = pl.BlockSpec((flat, block), lambda j: (0, jnp.minimum(j, steps - 1)))
    return pl.pallas_call(
        expert_kernel,
        grid=(steps + width // part,),
        out_shape=(
            pltpu.HBM((width, 2 * hid), BF16),
            pltpu.HBM((flat, hid), BF16),
            pltpu.HBM((flat, hid), BF16),
        ),
        in_specs=[VMEM, weight, weight],
        out_specs=[
            pl.BlockSpec((part, 2 * hid), lambda j: (jnp.maximum(j - steps, 0), 0)),
            hidden,
            hidden,
        ],
        scratch_shapes=[pltpu.VMEM((flat, hid), BF16)] * 2,
        compiler_params=params(30),
        cost_estimate=cost(8 * flat * width * hid, 12 * MIB),
        name="expert",
    )(moved, in_hbm(w_in), in_hbm(w_out))


def widen(total):
    rows, columns = total.shape
    return pl.pallas_call(
        widen_kernel,
        out_shape=[shape((rows, columns // 2), F32)] * 2,
        grid=(1,),
        in_specs=[pl.BlockSpec((rows, columns), lambda i: (0, 0))],
        out_specs=[pl.BlockSpec((rows, columns // 2), lambda i: (0, 0))] * 2,
        compiler_params=params(4),
        cost_estimate=cost(0, MIB),
        name="widen",
    )(in_hbm(total))


def return_rows(hidden, gh, w_in, w_out, sources):
    flat, hid = hidden.shape
    width = w_in.shape[0]
    block = 256
    count = flat // sources
    whole = pl.BlockSpec((flat, hid), lambda j: (0, 0), pipeline_mode=pl.Buffered(1))
    weight = pl.BlockSpec((block, hid), lambda j: (j, 0))
    return pl.pallas_call(
        return_kernel,
        grid=(width // block,),
        out_shape=pltpu.HBM((sources, 2, count, width), BF16),
        in_specs=[whole, whole, weight, weight],
        out_specs=pl.BlockSpec((sources, 2, count, block), lambda j: (0, 0, 0, j)),
        compiler_params=params(16),
        cost_estimate=cost(4 * flat * width * hid, 8 * MIB),
        name="return_rows",
    )(*(in_hbm(v) for v in (hidden, gh, w_in, w_out)))


SMEM = pl.BlockSpec(memory_space=pltpu.SMEM)


def place(where, pieces):
    dims = pieces[0].shape
    return pl.pallas_call(
        place_kernel,
        out_shape=shape((len(pieces),) + dims, BF16),
        in_specs=[SMEM] + [VMEM] * len(pieces),
        out_specs=VMEM,
        compiler_params=params(8),
        cost_estimate=cost(0, 4 * MIB),
        name="place",
    )(where, *pieces)


def exchange(rows, axes):
    return lax.all_to_all(rows, axes, split_axis=0, concat_axis=0, tiled=True)


def shifted(value, axis, k):
    n = lax.axis_size(axis)
    return lax.ppermute(value, axis, [(i, (i + k) % n) for i in range(n)])


def where_on(axis):
    return lax.axis_index(axis).astype(jnp.int32).reshape(1)


def gather_by(axis, piece):
    far, after, before = (shifted(piece, axis, k) for k in (2, 1, 3))
    return place(where_on(axis), [piece, after, far, before])


def gather_y(piece):
    parts = lax.axis_size("yh")
    return exchange(jnp.broadcast_to(piece[None], (parts,) + piece.shape), "yh")


def local(
    patches,
    expert_ids,
    gate_weights,
    conv_weight,
    conv_bias,
    ln_gain,
    ln_shift,
    w_in,
    w_out,
    grad_mixed,
):
    hid = w_in.shape[2]
    dp = ("x", "yh")
    ep = ("z", "yl", "core")
    full_in = lax.all_gather(w_in, dp, axis=1, tiled=True)[0]
    sent, xhat, rstd = send(
        expert_ids,
        gate_weights,
        grad_mixed,
        patches,
        conv_weight,
        conv_bias,
        ln_gain,
        ln_shift,
    )
    moved = exchange(sent, ep)
    along_y = gather_y(w_out[0])
    full_out = gather_by("x", along_y.reshape(-1, hid)).reshape(-1, hid)
    partial, hidden, gh = expert(moved, full_in, full_out)
    over_x = lax.psum_scatter(partial, "x", scatter_dimension=0, tiled=True)
    back = return_rows(hidden, gh, full_in, full_out, moved.shape[0])
    returned = exchange(back, ep)
    total = lax.psum_scatter(over_x, "yh", scatter_dimension=0, tiled=True)
    grad_in, grad_out = widen(total)
    mixed, grad_input = finish(
        expert_ids,
        gate_weights,
        returned,
        xhat,
        rstd,
        ln_gain,
        conv_weight,
        grad_mixed,
        patches,
    )
    return (mixed, grad_input, grad_in[None], grad_out[None])


def solution(mesh):
    fine = Mesh(mesh.devices.reshape(4, 4, 8, 2, 2), ("x", "yh", "z", "yl", "core"))
    dp = ("x", "yh")
    ep = ("z", "yl", "core")
    rows = P(dp + ep, None)
    weight = P(ep, dp, None)
    return jax.shard_map(
        local,
        mesh=fine,
        in_specs=(rows, rows, rows, P(), P(), P(), P(), weight, weight, rows),
        out_specs=(rows, rows, weight, weight),
        check_vma=False,
    )
```

```python
import jax
import jax.numpy as jnp
from jax import lax
from jax.experimental import pallas as pl
from jax.experimental.pallas import tpu as pltpu
from jax.sharding import Mesh, PartitionSpec as P


KSIZE = 7
TOP = 2
IMG_W = 16
IMG_H = 8
EPS = 1e-06
EXPERTS = 32
CAP = 16
TOK = 128
SLOTS = EXPERTS * CAP
LANES = 128
F32 = jnp.float32
BF16 = jnp.bfloat16
MIB = 1 << 20

VMEM = pl.BlockSpec(memory_space=pltpu.VMEM)


def dot(a, b):
    return jnp.dot(a, b, preferred_element_type=F32)


def iota(shape, dim):
    return lax.broadcasted_iota(jnp.int32, shape, dim)


def slot_selects(ids_ref):
    turned = [
        jnp.broadcast_to(ids_ref[:, k : k + 1].astype(F32), (TOK, TOK)).T.astype(jnp.int32)
        for k in range(TOP)
    ]
    hot = [row[:EXPERTS] == iota((EXPERTS, TOK), 0) for row in turned]
    table = (hot[0] | hot[1]).astype(F32).astype(BF16)
    before = (iota((TOK, TOK), 0) < iota((TOK, TOK), 1)).astype(F32).astype(BF16)
    earlier = dot(table, before)
    out = []
    for k in range(TOP):
        slot = jnp.sum(jnp.where(hot[k], earlier, 0.0), axis=0, keepdims=True)
        position = turned[k][:1] * CAP + slot.astype(jnp.int32)
        out.append(iota((SLOTS, TOK), 0) == position)
    return out


def patch_selects(ids_ref):
    hot = [ids_ref[:, k : k + 1] == iota((TOK, EXPERTS), 1) for k in range(TOP)]
    table = (hot[0] | hot[1]).astype(F32).astype(BF16)
    before = (iota((TOK, TOK), 1) < iota((TOK, TOK), 0)).astype(F32).astype(BF16)
    earlier = dot(before, table)
    out = []
    for k in range(TOP):
        slot = jnp.sum(jnp.where(hot[k], earlier, 0.0), axis=1, keepdims=True)
        position = ids_ref[:, k : k + 1] * CAP + slot.astype(jnp.int32)
        out.append(iota((TOK, SLOTS), 1) == position)
    return out


def as_bf16(mask):
    return mask.astype(F32).astype(BF16)


def depthwise(padded, taps_ref, flip, start, put):
    half = KSIZE // 2

    def chunk(c, _):
        lanes = pl.ds(pl.multiple_of(c * LANES, LANES), LANES)
        total = start(lanes)
        for col in range(KSIZE):
            begin = 8 + col - half
            shifted = padded[:, begin : begin + IMG_W, lanes]
            for row in range(KSIZE):
                tap = (KSIZE - 1 - row) * KSIZE + KSIZE - 1 - col if flip else row * KSIZE + col
                weight = taps_ref[tap : tap + 1, lanes]
                total = total + shifted[row : row + IMG_H] * weight[None]
        put(lanes, total)
        return 0

    lax.fori_loop(0, padded.shape[2] // LANES, chunk, 0)


def front_kernel(
    ids_ref,
    x_ref,
    taps_ref,
    bias_ref,
    gain_ref,
    shift_ref,
    sent_ref,
    xhat_ref,
    rstd_ref,
    padded,
    total,
):
    width = x_ref.shape[1]
    half = KSIZE // 2
    padded[...] = jnp.zeros_like(padded)
    padded[half : half + IMG_H, 8 : 8 + IMG_W, :] = (
        x_ref[...].astype(F32).reshape(IMG_H, IMG_W, width)
    )

    def start(lanes):
        return jnp.broadcast_to(bias_ref[:, lanes][None], (IMG_H, IMG_W, LANES))

    def put(lanes, value):
        total[:, lanes] = value.reshape(TOK, LANES)

    depthwise(padded, taps_ref, False, start, put)
    conv = total[...]
    mean = jnp.sum(conv, axis=1, keepdims=True) * (1.0 / width)
    centred = conv - mean
    spread = jnp.sum(centred * centred, axis=1, keepdims=True) * (1.0 / width)
    rstd = lax.rsqrt(spread + EPS)
    xhat = centred * rstd
    xhat_ref[...] = xhat
    rstd_ref[...] = jnp.broadcast_to(rstd, (TOK, LANES))
    normed = (xhat * gain_ref[...] + shift_ref[...]).astype(BF16)
    select = slot_selects(ids_ref)
    sent_ref[...] = dot(as_bf16(select[0] | select[1]), normed).astype(BF16)


def send_grads_kernel(ids_ref, gates_ref, cot_ref, out_ref):
    select = slot_selects(ids_ref)
    cot = cot_ref[...].astype(F32)
    first = (gates_ref[:, 0:1] * cot).astype(BF16)
    second = (gates_ref[:, 1:2] * cot).astype(BF16)
    out_ref[...] = (dot(as_bf16(select[0]), first) + dot(as_bf16(select[1]), second)).astype(BF16)


def finish_kernel(
    ids_ref,
    gates_ref,
    back_ref,
    xhat_ref,
    rstd_ref,
    gain_ref,
    taps_ref,
    cot_ref,
    x_ref,
    mixed_ref,
    out_ref,
    padded,
):
    width = xhat_ref.shape[1]
    half = KSIZE // 2
    select = [as_bf16(mask) for mask in patch_selects(ids_ref)]
    rows = back_ref[:, 1].reshape(SLOTS, width)
    combined = gates_ref[:, 0:1] * dot(select[0], rows)
    combined = combined + gates_ref[:, 1:2] * dot(select[1], rows)
    mixed_ref[...] = (x_ref[...].astype(F32) + combined).astype(BF16)

    grad = dot(select[0] + select[1], back_ref[:, 0].reshape(SLOTS, width))
    grad = grad * gain_ref[...]
    xhat = xhat_ref[...]
    mean = jnp.sum(grad, axis=1, keepdims=True) * (1.0 / width)
    along = jnp.sum(grad * xhat, axis=1, keepdims=True) * (1.0 / width)
    grad = rstd_ref[:, 0:1] * (grad - mean - xhat * along)
    padded[...] = jnp.zeros_like(padded)
    padded[half : half + IMG_H, 8 : 8 + IMG_W, :] = grad.reshape(IMG_H, IMG_W, width)

    def start(lanes):
        return jnp.zeros((IMG_H, IMG_W, LANES), F32)

    def put(lanes, value):
        out_ref[:, lanes] = cot_ref[:, lanes].astype(F32) + value.reshape(TOK, LANES)

    depthwise(padded, taps_ref, True, start, put)


def contract_last(left, right):
    return lax.dot_general(left, right, (((1,), (1,)), ((), ())), preferred_element_type=F32)


def contract_first(left, right):
    return lax.dot_general(left, right, (((0,), (0,)), ((), ())), preferred_element_type=F32)


SQRT_2_OVER_PI = 0.7978845608028654


def expert_kernel(
    rows_ref,
    grads_ref,
    w_in_ref,
    w_out_ref,
    terms_ref,
    hidden_ref,
    gh_ref,
    hidden_s,
    gh_s,
):
    step = pl.program_id(0)
    block = w_in_ref.shape[1]
    part = terms_ref.shape[0]
    steps = hidden_s.shape[1] // block

    @pl.when(step < steps)
    def _():
        pre = dot(rows_ref[...], w_in_ref[...])
        raw = dot(grads_ref[...], w_out_ref[...])
        square = pre * pre
        t = jnp.tanh(SQRT_2_OVER_PI * (pre + 0.044715 * (pre * square)))
        cdf = 0.5 * (1.0 + t)
        slope = cdf + pre * (0.5 * (1.0 - t * t)) * (
            SQRT_2_OVER_PI * (1.0 + (3 * 0.044715) * square)
        )
        lanes = pl.ds(pl.multiple_of(step * block, block), block)
        hidden = (pre * cdf).astype(BF16)
        gh = (raw * slope).astype(BF16)
        hidden_s[:, lanes] = hidden
        gh_s[:, lanes] = gh
        hidden_ref[...] = hidden
        gh_ref[...] = gh

    @pl.when(step >= steps)
    def _():
        lanes = pl.ds(pl.multiple_of((step - steps) * part, part), part)
        rows = rows_ref[:, lanes]
        grads = grads_ref[:, lanes]
        hid = hidden_s.shape[1]
        terms_ref[:, :hid] = contract_first(rows, gh_s[...]).astype(BF16)
        terms_ref[:, hid:] = contract_first(grads, hidden_s[...]).astype(BF16)


def return_kernel(hidden_ref, gh_ref, w_in_ref, w_out_ref, back_ref):
    sources, _, count, block = back_ref.shape
    grad = contract_last(gh_ref[...], w_in_ref[...]).astype(BF16)
    back_ref[:, 0] = grad.reshape(sources, count, block)
    out = contract_last(hidden_ref[...], w_out_ref[...]).astype(BF16)
    back_ref[:, 1] = out.reshape(sources, count, block)


def widen_kernel(sum_ref, in_ref, out_ref):
    hid = in_ref.shape[1]
    in_ref[...] = sum_ref[:, :hid].astype(F32)
    out_ref[...] = sum_ref[:, hid:].astype(F32)


def place_kernel(where_ref, *refs):
    pieces, out_ref = refs[:-1], refs[-1]
    for k, piece in enumerate(pieces):
        at = lax.rem(where_ref[0] + len(pieces) - k, len(pieces))
        out_ref[at] = piece[...]


def params(mib=16):
    return pltpu.CompilerParams(vmem_limit_bytes=mib * MIB)


def cost(flops, nbytes):
    return pl.CostEstimate(flops=int(flops), bytes_accessed=int(nbytes), transcendentals=0)


def shape(dims, dtype):
    return jax.ShapeDtypeStruct(dims, dtype)


def in_hbm(array):
    return pltpu.with_memory_space_constraint(array, pltpu.HBM)


def all_of(dims):
    return pl.BlockSpec(dims, lambda i: (0,) * len(dims))


def send_grads(ids, gates, cot):
    width = cot.shape[1]
    return pl.pallas_call(
        send_grads_kernel,
        grid=(1,),
        out_shape=pltpu.HBM((SLOTS, width), BF16),
        in_specs=[VMEM] * 2 + [all_of(cot.shape)],
        out_specs=all_of((SLOTS, width)),
        compiler_params=params(),
        cost_estimate=cost(4 * SLOTS * TOK * width, 2 * SLOTS * width),
        name="send_grads",
    )(ids, gates, in_hbm(cot))


def front(ids, x, taps, bias, gain, shift):
    width = x.shape[1]
    rows = [bias.reshape(1, width), gain.reshape(1, width), shift.reshape(1, width)]
    outs = [((SLOTS, width), BF16), ((TOK, width), F32), ((TOK, LANES), F32)]
    wide = [in_hbm(v) for v in (x, taps)]
    return pl.pallas_call(
        front_kernel,
        grid=(1,),
        out_shape=tuple(pltpu.HBM(*out) for out in outs),
        in_specs=[VMEM] + [all_of(v.shape) for v in wide] + [VMEM] * 3,
        out_specs=[all_of(dims) for dims, _ in outs],
        scratch_shapes=[
            pltpu.VMEM((IMG_H + KSIZE - 1, IMG_W + 16, width), F32),
            pltpu.VMEM((TOK, width), F32),
        ],
        compiler_params=params(20),
        cost_estimate=cost(100 * TOK * width * 20, 4 * SLOTS * width),
        name="front",
    )(ids, *wide, *rows)


def finish(ids, gates, back, xhat, rstd, gain, taps, cot, x):
    width = cot.shape[1]
    return pl.pallas_call(
        finish_kernel,
        out_shape=(shape((TOK, width), BF16), shape((TOK, width), F32)),
        in_specs=[VMEM] * 9,
        out_specs=[VMEM] * 2,
        scratch_shapes=[pltpu.VMEM((IMG_H + KSIZE - 1, IMG_W + 16, width), F32)],
        compiler_params=params(),
        cost_estimate=cost(100 * TOK * width * 20, 4 * SLOTS * width),
        name="finish",
    )(ids, gates, back, xhat, rstd, gain.reshape(1, width), taps, cot, x)


def expert(rows, grads, w_in, w_out):
    flat, width = rows.shape
    hid = w_in.shape[1]
    block = 512
    part = 256
    steps = hid // block
    weight = pl.BlockSpec((width, block), lambda j: (0, jnp.minimum(j, steps - 1)))
    hidden = pl.BlockSpec((flat, block), lambda j: (0, jnp.minimum(j, steps - 1)))
    return pl.pallas_call(
        expert_kernel,
        grid=(steps + width // part,),
        out_shape=(
            pltpu.HBM((width, 2 * hid), BF16),
            pltpu.HBM((flat, hid), BF16),
            pltpu.HBM((flat, hid), BF16),
        ),
        in_specs=[VMEM, VMEM, weight, weight],
        out_specs=[
            pl.BlockSpec((part, 2 * hid), lambda j: (jnp.maximum(j - steps, 0), 0)),
            hidden,
            hidden,
        ],
        scratch_shapes=[pltpu.VMEM((flat, hid), BF16)] * 2,
        compiler_params=params(30),
        cost_estimate=cost(8 * flat * width * hid, 12 * MIB),
        name="expert",
    )(rows, grads, in_hbm(w_in), in_hbm(w_out))


def widen(total):
    rows, columns = total.shape
    return pl.pallas_call(
        widen_kernel,
        out_shape=[shape((rows, columns // 2), F32)] * 2,
        grid=(1,),
        in_specs=[pl.BlockSpec((rows, columns), lambda i: (0, 0))],
        out_specs=[pl.BlockSpec((rows, columns // 2), lambda i: (0, 0))] * 2,
        compiler_params=params(4),
        cost_estimate=cost(0, MIB),
        name="widen",
    )(in_hbm(total))


def return_rows(hidden, gh, w_in, w_out, sources):
    flat, hid = hidden.shape
    width = w_in.shape[0]
    block = 256
    count = flat // sources
    whole = pl.BlockSpec((flat, hid), lambda j: (0, 0), pipeline_mode=pl.Buffered(1))
    weight = pl.BlockSpec((block, hid), lambda j: (j, 0))
    return pl.pallas_call(
        return_kernel,
        grid=(width // block,),
        out_shape=pltpu.HBM((sources, 2, count, width), BF16),
        in_specs=[whole, whole, weight, weight],
        out_specs=pl.BlockSpec((sources, 2, count, block), lambda j: (0, 0, 0, j)),
        compiler_params=params(16),
        cost_estimate=cost(4 * flat * width * hid, 8 * MIB),
        name="return_rows",
    )(*(in_hbm(v) for v in (hidden, gh, w_in, w_out)))


SMEM = pl.BlockSpec(memory_space=pltpu.SMEM)


def place(where, pieces):
    dims = pieces[0].shape
    return pl.pallas_call(
        place_kernel,
        out_shape=shape((len(pieces),) + dims, BF16),
        in_specs=[SMEM] + [VMEM] * len(pieces),
        out_specs=VMEM,
        compiler_params=params(8),
        cost_estimate=cost(0, 4 * MIB),
        name="place",
    )(where, *pieces)


def exchange(rows, axes):
    return lax.all_to_all(rows, axes, split_axis=0, concat_axis=0, tiled=True)


def exchange_rows(rows, axes):
    count, width = rows.shape
    return exchange(rows.reshape(EXPERTS, CAP, width), axes).reshape(count, width)


def shifted(value, axis, k):
    n = lax.axis_size(axis)
    return lax.ppermute(value, axis, [(i, (i + k) % n) for i in range(n)])


def where_on(axis):
    return lax.axis_index(axis).astype(jnp.int32).reshape(1)


def gather_by(axis, piece):
    far, after, before = (shifted(piece, axis, k) for k in (2, 1, 3))
    return place(where_on(axis), [piece, after, far, before])


def local(
    patches,
    expert_ids,
    gate_weights,
    conv_weight,
    conv_bias,
    ln_gain,
    ln_shift,
    w_in,
    w_out,
    grad_mixed,
):
    hid = w_in.shape[2]
    dp = ("x", "yh")
    ep = ("z", "yl", "core")
    full_in = lax.all_gather(w_in, dp, axis=1, tiled=True)[0]
    gated = send_grads(expert_ids, gate_weights, grad_mixed)
    grads = exchange_rows(gated, ep)
    along_y = gather_by("yh", w_out[0])
    sent, xhat, rstd = front(
        expert_ids, patches, conv_weight, conv_bias, ln_gain, ln_shift
    )
    rows = exchange_rows(sent, ep)
    full_out = gather_by("x", along_y.reshape(-1, hid)).reshape(-1, hid)
    partial, hidden, gh = expert(rows, grads, full_in, full_out)
    over_x = lax.psum_scatter(partial, "x", scatter_dimension=0, tiled=True)
    back = return_rows(hidden, gh, full_in, full_out, EXPERTS)
    returned = exchange(back, ep)
    total = lax.psum_scatter(over_x, "yh", scatter_dimension=0, tiled=True)
    grad_in, grad_out = widen(total)
    mixed, grad_input = finish(
        expert_ids,
        gate_weights,
        returned,
        xhat,
        rstd,
        ln_gain,
        conv_weight,
        grad_mixed,
        patches,
    )
    return (mixed, grad_input, grad_in[None], grad_out[None])


def solution(mesh):
    fine = Mesh(mesh.devices.reshape(4, 4, 8, 2, 2), ("x", "yh", "z", "yl", "core"))
    dp = ("x", "yh")
    ep = ("z", "yl", "core")
    rows = P(dp + ep, None)
    weight = P(ep, dp, None)
    return jax.shard_map(
        local,
        mesh=fine,
        in_specs=(rows, rows, rows, P(), P(), P(), P(), weight, weight, rows),
        out_specs=(rows, rows, weight, weight),
        check_vma=False,
    )
```

```python
import jax
import jax.numpy as jnp
from jax import lax
from jax.experimental import pallas as pl
from jax.experimental.pallas import tpu as pltpu
from jax.sharding import Mesh, PartitionSpec as P


KSIZE = 7
TOP = 2
IMG_W = 16
IMG_H = 8
EPS = 1e-06
EXPERTS = 32
CAP = 16
TOK = 128
SLOTS = EXPERTS * CAP
LANES = 128
F32 = jnp.float32
BF16 = jnp.bfloat16
MIB = 1 << 20

VMEM = pl.BlockSpec(memory_space=pltpu.VMEM)


def dot(a, b):
    return jnp.dot(a, b, preferred_element_type=F32)


def iota(shape, dim):
    return lax.broadcasted_iota(jnp.int32, shape, dim)


def slot_selects(ids_ref):
    turned = [
        jnp.broadcast_to(ids_ref[:, k : k + 1].astype(F32), (TOK, TOK)).T.astype(jnp.int32)
        for k in range(TOP)
    ]
    hot = [row[:EXPERTS] == iota((EXPERTS, TOK), 0) for row in turned]
    table = (hot[0] | hot[1]).astype(F32).astype(BF16)
    before = (iota((TOK, TOK), 0) < iota((TOK, TOK), 1)).astype(F32).astype(BF16)
    earlier = dot(table, before)
    out = []
    for k in range(TOP):
        slot = jnp.sum(jnp.where(hot[k], earlier, 0.0), axis=0, keepdims=True)
        position = turned[k][:1] * CAP + slot.astype(jnp.int32)
        out.append(iota((SLOTS, TOK), 0) == position)
    return out


def patch_selects(ids_ref):
    hot = [ids_ref[:, k : k + 1] == iota((TOK, EXPERTS), 1) for k in range(TOP)]
    table = (hot[0] | hot[1]).astype(F32).astype(BF16)
    before = (iota((TOK, TOK), 1) < iota((TOK, TOK), 0)).astype(F32).astype(BF16)
    earlier = dot(before, table)
    out = []
    for k in range(TOP):
        slot = jnp.sum(jnp.where(hot[k], earlier, 0.0), axis=1, keepdims=True)
        position = ids_ref[:, k : k + 1] * CAP + slot.astype(jnp.int32)
        out.append(iota((TOK, SLOTS), 1) == position)
    return out


def as_bf16(mask):
    return mask.astype(F32).astype(BF16)


def depthwise(padded, taps_ref, flip, start, put):
    half = KSIZE // 2

    def chunk(c, _):
        lanes = pl.ds(pl.multiple_of(c * LANES, LANES), LANES)
        total = start(lanes)
        for col in range(KSIZE):
            begin = 8 + col - half
            shifted = padded[:, begin : begin + IMG_W, lanes]
            for row in range(KSIZE):
                tap = (KSIZE - 1 - row) * KSIZE + KSIZE - 1 - col if flip else row * KSIZE + col
                weight = taps_ref[tap : tap + 1, lanes]
                total = total + shifted[row : row + IMG_H] * weight[None]
        put(lanes, total)
        return 0

    lax.fori_loop(0, padded.shape[2] // LANES, chunk, 0)


def send_kernel(
    ids_ref,
    gates_ref,
    cot_ref,
    x_ref,
    taps_ref,
    bias_ref,
    gain_ref,
    shift_ref,
    sent_ref,
    xhat_ref,
    rstd_ref,
    padded,
    total,
):
    width = x_ref.shape[1]
    half = KSIZE // 2
    padded[...] = jnp.zeros_like(padded)
    padded[half : half + IMG_H, 8 : 8 + IMG_W, :] = (
        x_ref[...].astype(F32).reshape(IMG_H, IMG_W, width)
    )

    def start(lanes):
        return jnp.broadcast_to(bias_ref[:, lanes][None], (IMG_H, IMG_W, LANES))

    def put(lanes, value):
        total[:, lanes] = value.reshape(TOK, LANES)

    depthwise(padded, taps_ref, False, start, put)
    conv = total[...]
    mean = jnp.sum(conv, axis=1, keepdims=True) * (1.0 / width)
    centred = conv - mean
    spread = jnp.sum(centred * centred, axis=1, keepdims=True) * (1.0 / width)
    rstd = lax.rsqrt(spread + EPS)
    xhat = centred * rstd
    xhat_ref[...] = xhat
    rstd_ref[...] = jnp.broadcast_to(rstd, (TOK, LANES))
    normed = (xhat * gain_ref[...] + shift_ref[...]).astype(BF16)
    select = slot_selects(ids_ref)
    sent = dot(as_bf16(select[0] | select[1]), normed).astype(BF16)
    sent_ref[:, 0] = sent.reshape(EXPERTS, CAP, width)
    cot = cot_ref[...].astype(F32)
    first = (gates_ref[:, 0:1] * cot).astype(BF16)
    second = (gates_ref[:, 1:2] * cot).astype(BF16)
    sent = (dot(as_bf16(select[0]), first) + dot(as_bf16(select[1]), second)).astype(BF16)
    sent_ref[:, 1] = sent.reshape(EXPERTS, CAP, width)


def finish_kernel(
    ids_ref,
    gates_ref,
    back_ref,
    xhat_ref,
    rstd_ref,
    gain_ref,
    taps_ref,
    cot_ref,
    x_ref,
    mixed_ref,
    out_ref,
    padded,
):
    width = xhat_ref.shape[1]
    half = KSIZE // 2
    select = [as_bf16(mask) for mask in patch_selects(ids_ref)]
    rows = back_ref[:, 1].reshape(SLOTS, width)
    combined = gates_ref[:, 0:1] * dot(select[0], rows)
    combined = combined + gates_ref[:, 1:2] * dot(select[1], rows)
    mixed_ref[...] = (x_ref[...].astype(F32) + combined).astype(BF16)

    grad = dot(select[0] + select[1], back_ref[:, 0].reshape(SLOTS, width))
    grad = grad * gain_ref[...]
    xhat = xhat_ref[...]
    mean = jnp.sum(grad, axis=1, keepdims=True) * (1.0 / width)
    along = jnp.sum(grad * xhat, axis=1, keepdims=True) * (1.0 / width)
    grad = rstd_ref[:, 0:1] * (grad - mean - xhat * along)
    padded[...] = jnp.zeros_like(padded)
    padded[half : half + IMG_H, 8 : 8 + IMG_W, :] = grad.reshape(IMG_H, IMG_W, width)

    def start(lanes):
        return jnp.zeros((IMG_H, IMG_W, LANES), F32)

    def put(lanes, value):
        out_ref[:, lanes] = cot_ref[:, lanes].astype(F32) + value.reshape(TOK, LANES)

    depthwise(padded, taps_ref, True, start, put)


def contract_last(left, right):
    return lax.dot_general(left, right, (((1,), (1,)), ((), ())), preferred_element_type=F32)


def contract_first(left, right):
    return lax.dot_general(left, right, (((0,), (0,)), ((), ())), preferred_element_type=F32)


SQRT_2_OVER_PI = 0.7978845608028654


def expert_kernel(
    moved_ref,
    w_in_ref,
    w_out_ref,
    terms_ref,
    hidden_ref,
    gh_ref,
    hidden_s,
    gh_s,
):
    step = pl.program_id(0)
    sources, _, count, width = moved_ref.shape
    flat = sources * count
    block = w_in_ref.shape[1]
    part = terms_ref.shape[0]
    steps = hidden_s.shape[1] // block

    @pl.when(step < steps)
    def _():
        pre = dot(moved_ref[:, 0].reshape(flat, width), w_in_ref[...])
        raw = dot(moved_ref[:, 1].reshape(flat, width), w_out_ref[...])
        square = pre * pre
        t = jnp.tanh(SQRT_2_OVER_PI * (pre + 0.044715 * (pre * square)))
        cdf = 0.5 * (1.0 + t)
        slope = cdf + pre * (0.5 * (1.0 - t * t)) * (
            SQRT_2_OVER_PI * (1.0 + (3 * 0.044715) * square)
        )
        lanes = pl.ds(pl.multiple_of(step * block, block), block)
        hidden = (pre * cdf).astype(BF16)
        gh = (raw * slope).astype(BF16)
        hidden_s[:, lanes] = hidden
        gh_s[:, lanes] = gh
        hidden_ref[...] = hidden
        gh_ref[...] = gh

    @pl.when(step >= steps)
    def _():
        lanes = pl.ds(pl.multiple_of((step - steps) * part, part), part)
        rows = moved_ref[:, 0, :, lanes].reshape(flat, part)
        grads = moved_ref[:, 1, :, lanes].reshape(flat, part)
        hid = hidden_s.shape[1]
        terms_ref[:, :hid] = contract_first(rows, gh_s[...]).astype(BF16)
        terms_ref[:, hid:] = contract_first(grads, hidden_s[...]).astype(BF16)


def return_kernel(hidden_ref, gh_ref, w_in_ref, w_out_ref, back_ref):
    sources, _, count, block = back_ref.shape
    grad = contract_last(gh_ref[...], w_in_ref[...]).astype(BF16)
    back_ref[:, 0] = grad.reshape(sources, count, block)
    out = contract_last(hidden_ref[...], w_out_ref[...]).astype(BF16)
    back_ref[:, 1] = out.reshape(sources, count, block)


def widen_kernel(sum_ref, in_ref, out_ref):
    hid = in_ref.shape[1]
    in_ref[...] = sum_ref[:, :hid].astype(F32)
    out_ref[...] = sum_ref[:, hid:].astype(F32)


def repeat_kernel(piece_ref, out_ref):
    for k in range(out_ref.shape[0]):
        out_ref[k] = piece_ref[...]


def place_kernel(where_ref, *refs):
    pieces, out_ref = refs[:-1], refs[-1]
    for k, piece in enumerate(pieces):
        at = lax.rem(where_ref[0] + len(pieces) - k, len(pieces))
        out_ref[at] = piece[...]


def params(mib=16):
    return pltpu.CompilerParams(vmem_limit_bytes=mib * MIB)


def cost(flops, nbytes):
    return pl.CostEstimate(flops=int(flops), bytes_accessed=int(nbytes), transcendentals=0)


def shape(dims, dtype):
    return jax.ShapeDtypeStruct(dims, dtype)


def in_hbm(array):
    return pltpu.with_memory_space_constraint(array, pltpu.HBM)


def all_of(dims):
    return pl.BlockSpec(dims, lambda i: (0,) * len(dims))


def send(ids, gates, cot, x, taps, bias, gain, shift):
    width = x.shape[1]
    rows = [bias.reshape(1, width), gain.reshape(1, width), shift.reshape(1, width)]
    outs = [((EXPERTS, 2, CAP, width), BF16), ((TOK, width), F32), ((TOK, LANES), F32)]
    wide = [in_hbm(v) for v in (cot, x, taps)]
    return pl.pallas_call(
        send_kernel,
        grid=(1,),
        out_shape=tuple(pltpu.HBM(*out) for out in outs),
        in_specs=[VMEM] * 2 + [all_of(v.shape) for v in wide] + [VMEM] * 3,
        out_specs=[all_of(dims) for dims, _ in outs],
        scratch_shapes=[
            pltpu.VMEM((IMG_H + KSIZE - 1, IMG_W + 16, width), F32),
            pltpu.VMEM((TOK, width), F32),
        ],
        compiler_params=params(20),
        cost_estimate=cost(100 * TOK * width * 20, 4 * SLOTS * width),
        name="send",
    )(ids, gates, *wide, *rows)


def finish(ids, gates, back, xhat, rstd, gain, taps, cot, x):
    width = cot.shape[1]
    return pl.pallas_call(
        finish_kernel,
        out_shape=(shape((TOK, width), BF16), shape((TOK, width), F32)),
        in_specs=[VMEM] * 9,
        out_specs=[VMEM] * 2,
        scratch_shapes=[pltpu.VMEM((IMG_H + KSIZE - 1, IMG_W + 16, width), F32)],
        compiler_params=params(),
        cost_estimate=cost(100 * TOK * width * 20, 4 * SLOTS * width),
        name="finish",
    )(ids, gates, back, xhat, rstd, gain.reshape(1, width), taps, cot, x)


def expert(moved, w_in, w_out):
    sources, _, count, width = moved.shape
    flat = sources * count
    hid = w_in.shape[1]
    block = 512
    part = 256
    steps = hid // block
    weight = pl.BlockSpec((width, block), lambda j: (0, jnp.minimum(j, steps - 1)))
    hidden = pl.BlockSpec((flat, block), lambda j: (0, jnp.minimum(j, steps - 1)))
    return pl.pallas_call(
        expert_kernel,
        grid=(steps + width // part,),
        out_shape=(
            pltpu.HBM((width, 2 * hid), BF16),
            pltpu.HBM((flat, hid), BF16),
            pltpu.HBM((flat, hid), BF16),
        ),
        in_specs=[VMEM, weight, weight],
        out_specs=[
            pl.BlockSpec((part, 2 * hid), lambda j: (jnp.maximum(j - steps, 0), 0)),
            hidden,
            hidden,
        ],
        scratch_shapes=[pltpu.VMEM((flat, hid), BF16)] * 2,
        compiler_params=params(30),
        cost_estimate=cost(8 * flat * width * hid, 12 * MIB),
        name="expert",
    )(moved, in_hbm(w_in), in_hbm(w_out))


def widen(total):
    rows, columns = total.shape
    return pl.pallas_call(
        widen_kernel,
        out_shape=[shape((rows, columns // 2), F32)] * 2,
        grid=(1,),
        in_specs=[pl.BlockSpec((rows, columns), lambda i: (0, 0))],
        out_specs=[pl.BlockSpec((rows, columns // 2), lambda i: (0, 0))] * 2,
        compiler_params=params(4),
        cost_estimate=cost(0, MIB),
        name="widen",
    )(in_hbm(total))


def return_rows(hidden, gh, w_in, w_out, sources):
    flat, hid = hidden.shape
    width = w_in.shape[0]
    block = 256
    count = flat // sources
    whole = pl.BlockSpec((flat, hid), lambda j: (0, 0), pipeline_mode=pl.Buffered(1))
    weight = pl.BlockSpec((block, hid), lambda j: (j, 0))
    return pl.pallas_call(
        return_kernel,
        grid=(width // block,),
        out_shape=pltpu.HBM((sources, 2, count, width), BF16),
        in_specs=[whole, whole, weight, weight],
        out_specs=pl.BlockSpec((sources, 2, count, block), lambda j: (0, 0, 0, j)),
        compiler_params=params(16),
        cost_estimate=cost(4 * flat * width * hid, 8 * MIB),
        name="return_rows",
    )(*(in_hbm(v) for v in (hidden, gh, w_in, w_out)))


SMEM = pl.BlockSpec(memory_space=pltpu.SMEM)


def place(where, pieces):
    dims = pieces[0].shape
    return pl.pallas_call(
        place_kernel,
        out_shape=shape((len(pieces),) + dims, BF16),
        in_specs=[SMEM] + [VMEM] * len(pieces),
        out_specs=VMEM,
        compiler_params=params(8),
        cost_estimate=cost(0, 4 * MIB),
        name="place",
    )(where, *pieces)


def exchange(rows, axes):
    return lax.all_to_all(rows, axes, split_axis=0, concat_axis=0, tiled=True)


def shifted(value, axis, k):
    n = lax.axis_size(axis)
    return lax.ppermute(value, axis, [(i, (i + k) % n) for i in range(n)])


def where_on(axis):
    return lax.axis_index(axis).astype(jnp.int32).reshape(1)


def gather_by(axis, piece):
    far, after, before = (shifted(piece, axis, k) for k in (2, 1, 3))
    return place(where_on(axis), [piece, after, far, before])


def gather_y(piece):
    parts = lax.axis_size("yh")
    dims = (parts,) + piece.shape
    copies = pl.pallas_call(
        repeat_kernel,
        grid=(1,),
        out_shape=pltpu.HBM(dims, BF16),
        in_specs=[all_of(piece.shape)],
        out_specs=all_of(dims),
        compiler_params=params(4),
        cost_estimate=cost(0, MIB),
        name="repeat",
    )(in_hbm(piece))
    return exchange(copies, "yh")


def local(
    patches,
    expert_ids,
    gate_weights,
    conv_weight,
    conv_bias,
    ln_gain,
    ln_shift,
    w_in,
    w_out,
    grad_mixed,
):
    hid = w_in.shape[2]
    dp = ("x", "yh")
    ep = ("z", "yl", "core")
    full_in = lax.all_gather(w_in, dp, axis=1, tiled=True)[0]
    sent, xhat, rstd = send(
        expert_ids,
        gate_weights,
        grad_mixed,
        patches,
        conv_weight,
        conv_bias,
        ln_gain,
        ln_shift,
    )
    moved = exchange(sent, ep)
    along_y = gather_y(w_out[0])
    full_out = gather_by("x", along_y.reshape(-1, hid)).reshape(-1, hid)
    partial, hidden, gh = expert(moved, full_in, full_out)
    over_x = lax.psum_scatter(partial, "x", scatter_dimension=0, tiled=True)
    back = return_rows(hidden, gh, full_in, full_out, moved.shape[0])
    returned = exchange(back, ep)
    total = lax.psum_scatter(over_x, "yh", scatter_dimension=0, tiled=True)
    grad_in, grad_out = widen(total)
    mixed, grad_input = finish(
        expert_ids,
        gate_weights,
        returned,
        xhat,
        rstd,
        ln_gain,
        conv_weight,
        grad_mixed,
        patches,
    )
    return (mixed, grad_input, grad_in[None], grad_out[None])


def solution(mesh):
    fine = Mesh(mesh.devices.reshape(4, 4, 8, 2, 2), ("x", "yh", "z", "yl", "core"))
    dp = ("x", "yh")
    ep = ("z", "yl", "core")
    rows = P(dp + ep, None)
    weight = P(ep, dp, None)
    return jax.shard_map(
        local,
        mesh=fine,
        in_specs=(rows, rows, rows, P(), P(), P(), P(), weight, weight, rows),
        out_specs=(rows, rows, weight, weight),
        check_vma=False,
    )
```
